32 devices in a mesh: band: 4 (over x, core), space: 8 (over z, y).
Axes of the slice: x: 2, y: 2, z: 4, core: 2. Of those that a mesh axis runs over, the one named last changes fastest.
Arguments:
- orbitals: bfloat16 [96, 128, 16, 128], P('band', 'space'), may hold values from -0.796875 to 0.796875
- occupations: float32 [96], P('band'), may hold values from 0.5 to 2
- potential_in: float32 [128, 16, 128], P('space'), may hold values from -6 to 6
- ionic_potential: float32 [128, 16, 128], P('space'), may hold values from -6 to 6
- hartree_prev: float32 [128, 16, 128], P('space'), may hold values from -6 to 6
- projectors: bfloat16 [64, 13, 16, 256], P('space'), may hold values from -0.375 to 0.375
- box_start: int32 [3, 64], replicated, may hold values from 0 to 127, as said below
- coupling: float32 [13, 13], replicated, may hold values from -6 to 6
Outputs:
- applied: bfloat16 [96, 128, 16, 128], P('band', 'space')
- potential: float32 [128, 16, 128], P('space')
The draws below stay inside these ranges and needn't reach their ends.
Inputs may be any that keep to these rules, and one draw needn't show every extreme that they name: `box_start`: column a holds the first plane, row and column of atom a's box. The plane lies among the 16 planes that begin at (a // 8) * 16; the row is at most 0 and the column at most 112. Atom 0's box begins at plane, row and column 0, and the last atom's box begins on plane 128 - 1.
All inputs are finite; a program needn't handle non-finite values.
Results may differ from the reference program's by a relative error of at most 0.013.
Values may be sent and summed in bfloat16 or wider, within the bound.
No kernel may reach another device: no remote copies, remote signals or barrier semaphores. Data moves between devices by JAX's collectives and lax.ppermute only.
A program may use at most 128 MiB of HBM per device.

```python
import math
import jax
import jax.numpy as jnp
from jax import lax

NORB = 96
NPROJ = 13
BOX = 16
PLANES = 16
NY = 16
NZ = 128
ATOM_DEV = 8
SWEEPS = 2
NX = 128
ATOMS = 64


def draw_box_start(key, part):
    key_plane, key_row, key_col = jax.random.split(key, 3)
    atom_index = jnp.arange(ATOMS, dtype=jnp.int32)
    owners = atom_index // ATOM_DEV
    offset = jax.random.randint(key_plane, (ATOMS,), 0, PLANES, dtype=jnp.int32)
    offset = jnp.where(atom_index == 0, 0, jnp.where(atom_index == ATOMS - 1, PLANES - 1, offset))
    row_start = jax.random.randint(key_row, (ATOMS,), 0, NY - BOX + 1, dtype=jnp.int32)
    row_start = jnp.where(atom_index == 0, 0, row_start)
    col_start = jax.random.randint(key_col, (ATOMS,), 0, NZ - BOX + 1, dtype=jnp.int32)
    col_start = jnp.where(atom_index == 0, 0, col_start)
    return jnp.stack([owners * PLANES + offset, row_start, col_start]).astype(jnp.int32)


def levels(rng, extent, cuts, smallest, top_value):
    def one(position, parts):
        heights = jax.random.uniform(jax.random.fold_in(jax.random.fold_in(rng, 6), position), (parts,), jnp.float32, smallest / len(cuts), top_value / len(cuts))
        return jnp.repeat(jnp.exp(heights), extent[position] // parts).reshape((-1,) + (1,) * (len(extent) - position - 1))

    gain = one(*cuts[0])
    for cut in cuts[1:]:
        gain = gain * one(*cut)
    return gain


def centred(stream_key, dims, deviation, reach, cuts=(), kind=jnp.bfloat16):
    loudness = levels(stream_key, dims, cuts, -0.22, 0.18) if cuts else 1.0
    values = jax.random.normal(stream_key, dims, jnp.float32) * deviation * loudness
    return jnp.minimum(jnp.maximum(values, -reach), reach).astype(kind)


def setup_inputs(seed: int = 0) -> dict:
    keys = jax.random.split(jax.random.key(seed), 9)
    return {
        "orbitals": centred(keys[0], (NORB, NX, NY, NZ), 0.1, 0.796875, ((0, 4), (1, 8))),
        "occupations": jnp.clip(0.5 + 1.5 * jax.random.uniform(keys[1], (NORB,), jnp.float32) ** levels(keys[1], (NORB,), ((0, 4),), -0.2, 0.2), 0.5, 2.0),
        "potential_in": centred(keys[2], (NX, NY, NZ), 1.0, 6.0, ((0, 8),), jnp.float32),
        "ionic_potential": centred(keys[3], (NX, NY, NZ), 1.0, 6.0, ((0, 8),), jnp.float32),
        "hartree_prev": centred(keys[4], (NX, NY, NZ), 1.0, 6.0, ((0, 8),), jnp.float32),
        "projectors": centred(keys[5], (ATOMS, NPROJ, BOX, BOX * BOX), (BOX * BOX) ** -0.5, 0.375, ((0, 8),)),
        "box_start": draw_box_start(jax.random.fold_in(keys[8], 71), 0),
        "coupling": centred(keys[7], (NPROJ, NPROJ), 1.0, 6.0, (), jnp.float32),
    }


screening = 0.25
stencil_far = ((1, 4.0 / 3.0), (2, -1.0 / 12.0))


def fourth_order(field):
    summed = -7.5 * field
    for distance, weight in stencil_far:
        for dimension in (0, 1, 2):
            summed = summed + weight * (jnp.roll(field, distance, dimension) + jnp.roll(field, -distance, dimension))
    return summed


def reference(orbitals, occupations, potential_in, ionic_potential, hartree_prev, projectors, box_start, coupling):
    steps_box = jnp.arange(BOX, dtype=jnp.int32)
    plane_index = (box_start[0][:, None] + steps_box[None, :]) % NX
    row_index = box_start[1][:, None] + steps_box[None, :]
    col_index = box_start[2][:, None] + steps_box[None, :]
    linear = (plane_index[:, :, None, None] * NY + row_index[:, None, :, None]) * NZ + col_index[:, None, None, :]
    linear = linear.reshape(ATOMS, BOX, BOX * BOX).astype(jnp.int32)
    flat_index = linear.reshape(-1)
    beta_wide = projectors.astype(jnp.float32)
    coupling_wide = coupling.astype(jnp.float32)

    def per_orbital(density, inputs):
        orbital, weight = inputs
        field = orbital.astype(jnp.float32)
        local_part = -0.5 * fourth_order(field) + potential_in * field
        boxes = orbital.reshape(-1)[linear].astype(jnp.float32)
        coefficients = jnp.einsum("apxk,axk->ap", beta_wide, boxes)
        weighted = jnp.dot(coefficients, coupling_wide.T, precision=lax.Precision.HIGHEST).astype(jnp.bfloat16)
        weighted = lax.optimization_barrier(weighted).astype(jnp.float32)
        contrib = jnp.einsum("apxk,ap->axk", beta_wide, weighted)
        nonlocal_part = jnp.zeros((NX * NY * NZ,), jnp.float32).at[flat_index].add(contrib.reshape(-1))
        applied_one = (local_part + nonlocal_part.reshape(NX, NY, NZ)).astype(jnp.bfloat16)
        density = density + weight * field * field
        return density, applied_one

    density, applied = lax.scan(per_orbital, jnp.zeros((NX, NY, NZ), jnp.float32), (orbitals, occupations.astype(jnp.float32)))
    mean_density = jnp.mean(density)
    source = 4.0 * math.pi * (density - mean_density)
    hartree = hartree_prev
    for sweep_index in range(SWEEPS):
        neighbours = jnp.zeros_like(hartree)
        for dimension in (0, 1, 2):
            neighbours = neighbours + jnp.roll(hartree, 1, dimension) + jnp.roll(hartree, -1, dimension)
        hartree = (neighbours + source) / (6.0 + screening)
    potential = ionic_potential + hartree - jnp.cbrt(3.0 * density / math.pi)
    return applied, potential
```

```python
import functools
import math

import jax
import jax.numpy as jnp
import numpy as np
from jax import lax
from jax.experimental import pallas as pl
from jax.experimental.pallas import tpu as pltpu
from jax.sharding import PartitionSpec as P

SWEEPS = 2
LANES = 128
SLOT = 16

screening = 0.25
four_pi = 4.0 * math.pi
f32 = jnp.float32
bf16 = jnp.bfloat16


def vmem():
    return pl.BlockSpec(memory_space=pltpu.VMEM)


def smem():
    return pl.BlockSpec(memory_space=pltpu.SMEM)


def hbm():
    return pl.BlockSpec(memory_space=pl.ANY)


def spread_projectors(raw, atom, rows_ref):
    nproj, box, square = raw.shape
    flat = raw.reshape(nproj * box, square).astype(f32)
    for tile in range(square // LANES):
        rows_ref[atom, tile, : nproj * box] = flat[:, tile * LANES : (tile + 1) * LANES]
        rows_ref[atom, tile, nproj * box :] = jnp.zeros(
            (rows_ref.shape[2] - nproj * box, LANES), f32
        )


def place_plane(rows_ref, starts, plane, placed_ref, carried):
    atoms = rows_ref.shape[0]
    box = rows_ref.shape[2] // SLOT
    per_tile = LANES // box
    lane = lax.broadcasted_iota(jnp.int32, (SLOT, LANES), 1)

    def one(atom, _):
        offset = starts[0, atom]
        column = starts[1, atom]
        j = plane - offset
        if carried:
            j = j + box
        valid = jnp.logical_and(j >= 0, j < box)
        j = jnp.clip(j, 0, box - 1)
        low = jnp.where(valid, column, LANES)
        inside = jnp.logical_and(lane >= low, lane < low + box)
        for tile in range(box // per_tile):
            cells = rows_ref[atom, tile, pl.ds(j, SLOT, stride=box), :]
            for row in range(per_tile):
                shift = lax.rem(column + (LANES - box * row), LANES)
                moved = pltpu.roll(cells, shift, 1)
                placed_ref[
                    pl.ds(pl.multiple_of(atom * SLOT, SLOT), SLOT),
                    pl.ds((tile * per_tile + row) * LANES, LANES),
                ] = jnp.where(inside, moved, 0.0).astype(bf16)
        return 0

    lax.fori_loop(0, atoms, one, 0)


def turn_plane(field_ref, plane, wide_ref):
    count, _, rows, _ = field_ref.shape
    cells = field_ref[:, plane].astype(f32)
    wide_ref[...] = cells.reshape(count * rows, LANES)
    return jnp.concatenate(
        [wide_ref[pl.ds(r, count, stride=rows), :] for r in range(rows)], axis=1
    ).astype(bf16)


NT = (((1,), (1,)), ((), ()))


def density_kernel(occ, field_ref, out_ref):
    total = jnp.zeros(out_ref.shape, f32)
    for o in range(field_ref.shape[0]):
        cells = field_ref[o].astype(f32)
        total = total + (occ[o] * cells) * cells
    out_ref[...] = total


def coefficient_kernel(carried, starts, core, field_ref, *rest):
    if carried:
        mine_ref, other_ref, out_ref, rows_ref, placed_ref, wide_ref = rest
        half = mine_ref.shape[0]
        for q in range(half):
            spread_projectors(mine_ref[q], core[0] * half + q, rows_ref)
            spread_projectors(other_ref[q], (1 - core[0]) * half + q, rows_ref)
    else:
        proj_ref, out_ref, rows_ref, placed_ref, wide_ref = rest
        for q in range(proj_ref.shape[0]):
            spread_projectors(proj_ref[q], q, rows_ref)
    planes = field_ref.shape[1]
    out_ref[...] = jnp.zeros(out_ref.shape, f32)

    def one(plane, _):
        place_plane(rows_ref, starts, plane, placed_ref, carried)
        turned = turn_plane(field_ref, plane, wide_ref)
        out_ref[...] += lax.dot_general(
            turned, placed_ref[...], NT, preferred_element_type=f32
        )
        return 0

    lax.fori_loop(0, planes, one, 0)


def weigh(coef, coupling_ref):
    return lax.dot_general(
        coef, coupling_ref[...], (((1,), (0,)), ((), ())),
        precision=lax.Precision.HIGHEST, preferred_element_type=f32,
    ).astype(bf16)


def deposit(rows_ref, starts, weighted, placed_ref, sum_ref, planes, carried):
    count = weighted.shape[0]
    rows = placed_ref.shape[1] // LANES

    def one(plane, _):
        place_plane(rows_ref, starts, plane, placed_ref, carried)
        update = jnp.dot(weighted, placed_ref[...], preferred_element_type=f32)
        for r in range(rows):
            sum_ref[pl.ds(plane * rows + r, count, stride=planes * rows), :] = update[
                :, r * LANES : (r + 1) * LANES
            ]
        return 0

    lax.fori_loop(0, planes, one, 0)


def local_kernel(
    starts, core, field_ref, low_ref, high_ref, mine_ref, other_ref, part_ref, far_ref,
    coupling_ref, along_ref, across_ref, pot_ref, out_ref,
    rows_ref, placed_ref, sum_ref, ext_ref, sems,
):
    count, planes, rows, _ = field_ref.shape
    copies = [
        pltpu.make_async_copy(low_ref, ext_ref.at[:, 0:2], sems.at[0]),
        pltpu.make_async_copy(field_ref, ext_ref.at[:, 2 : 2 + planes], sems.at[1]),
        pltpu.make_async_copy(high_ref, ext_ref.at[:, 2 + planes : 4 + planes], sems.at[2]),
    ]
    for copy in copies:
        copy.start()
    half = mine_ref.shape[0]
    for q in range(half):
        spread_projectors(mine_ref[q], core[0] * half + q, rows_ref)
        spread_projectors(other_ref[q], (1 - core[0]) * half + q, rows_ref)
    weighted = weigh(part_ref[...] + far_ref[...], coupling_ref)
    deposit(rows_ref, starts, weighted, placed_ref, sum_ref, planes, True)
    for copy in copies:
        copy.wait()
    cells = planes * rows

    def one(o, _):
        ext = ext_ref[o].reshape((planes + 4) * rows, LANES)
        center = ext[2 * rows : 2 * rows + cells]
        stencil = jnp.dot(across_ref[...], ext, preferred_element_type=f32)
        stencil = stencil + jnp.dot(center, along_ref[...], preferred_element_type=f32)
        value = stencil * (-1.0 / 24.0) + pot_ref[...].reshape(cells, LANES) * center.astype(f32)
        nonlocal_part = sum_ref[pl.ds(pl.multiple_of(o * cells, cells), cells), :]
        out_ref[o] = (value + nonlocal_part).reshape(planes, rows, LANES)
        return 0

    lax.fori_loop(0, count, one, 0)


def final_kernel(
    starts, charge, acc_ref, proj_ref, part_ref, far_ref, coupling_ref,
    dens_ref, hart_ref, ionic_ref, below_ref, above_ref,
    out_ref, pot_ref, rows_ref, placed_ref, sum_ref,
):
    count, planes, rows, _ = out_ref.shape
    cells = planes * rows
    for q in range(proj_ref.shape[0]):
        spread_projectors(proj_ref[q], q, rows_ref)
    weighted = weigh(part_ref[...] + far_ref[:count], coupling_ref)
    deposit(rows_ref, starts, weighted, placed_ref, sum_ref, planes, False)

    def one(o, _):
        nonlocal_part = sum_ref[pl.ds(pl.multiple_of(o * cells, cells), cells), :]
        out_ref[o] = (acc_ref[o].reshape(cells, LANES) + nonlocal_part).reshape(
            planes, rows, LANES
        ).astype(bf16)
        return 0

    lax.fori_loop(0, count, one, 0)

    wide = planes + 4
    field = jnp.concatenate(
        [
            below_ref[count : count + 2 * rows].reshape(2, rows, LANES),
            hart_ref[...],
            above_ref[count : count + 2 * rows].reshape(2, rows, LANES),
        ],
        axis=0,
    )
    dens = jnp.concatenate(
        [
            below_ref[count + 2 * rows :].reshape(1, rows, LANES),
            dens_ref[...],
            above_ref[count + 2 * rows :].reshape(1, rows, LANES),
        ],
        axis=0,
    )
    source = four_pi * dens
    scale = 1.0 / (6.0 + screening)

    def relax(h, s):
        inner = h[1:-1]
        size = inner.shape
        flat = inner.reshape(size[0] * rows, LANES)
        across = pltpu.roll(flat, 1, 1) + pltpu.roll(flat, LANES - 1, 1)
        total = h[2:] + h[:-2] + across.reshape(size)
        total = total + pltpu.roll(inner, 1, 1) + pltpu.roll(inner, rows - 1, 1)
        return (total + s) * scale

    once = relax(field, source)
    twice = relax(once, source[1:-1])
    shift = charge[0] * (four_pi * scale * (1.0 + 6.0 * scale))
    third = (3.0 / math.pi) * dens_ref[...]
    root = jnp.exp(jnp.log(jnp.maximum(third, 1e-37)) * (1.0 / 3.0))
    root = (2.0 * root + third / jnp.maximum(root * root, 1e-30)) * (1.0 / 3.0)
    root = jnp.where(third > 0.0, root, 0.0)
    pot_ref[...] = ionic_ref[...] + twice - shift - root


def stencils(planes, rows):
    across = np.zeros((planes * rows, (planes + 4) * rows), np.float32)
    index = np.arange(planes * rows)
    plane, row = index // rows, index % rows
    for step, weight in ((1, 16.0), (2, -1.0)):
        for sign in (1, -1):
            np.add.at(across, (index, (plane + 2 + sign * step) * rows + row), weight)
            np.add.at(across, (index, (plane + 2) * rows + (row + sign * step) % rows), weight)
    along = np.zeros((LANES, LANES), np.float32)
    lane = np.arange(LANES)
    along[lane, lane] = -90.0
    for step, weight in ((1, 16.0), (2, -1.0)):
        for sign in (1, -1):
            np.add.at(along, ((lane + sign * step) % LANES, lane), weight)
    return jnp.asarray(across, bf16), jnp.asarray(along, bf16)


def around(block, axis, distance):
    count = lax.axis_size(axis)
    return lax.ppermute(block, axis, [(i, (i + distance) % count) for i in range(count)])


def swap(block, axis, mask):
    return lax.ppermute(block, axis, [(i, i ^ mask) for i in range(lax.axis_size(axis))])


def local(
    orbitals, occupations, potential_in, ionic_potential, hartree_prev, projectors, box_start, coupling
):
    count, planes, rows, lanes = orbitals.shape
    atoms, nproj, box, square = projectors.shape
    n_space = lax.axis_size("space")
    n_band = lax.axis_size("band")
    domain = lax.axis_index("space")
    core = lax.axis_index("band") % 2
    half = atoms // 2
    slots = atoms * SLOT
    params = functools.partial(pltpu.CompilerParams, vmem_limit_bytes=48 << 20)

    mine = around(lax.dynamic_slice_in_dim(projectors, core * half, half, 0), "space", 1)
    other = swap(mine, "band", 1)
    low = around(orbitals[:, planes - 2 :], "space", 1)
    high = around(orbitals[:, :2], "space", -1)

    behind = (domain + n_space - 1) % n_space
    own_starts = lax.dynamic_slice_in_dim(box_start, domain * atoms, atoms, 1)
    own_starts = jnp.stack([own_starts[0] % planes, own_starts[2]])
    prev_starts = lax.dynamic_slice_in_dim(box_start, behind * atoms, atoms, 1)
    prev_starts = jnp.stack([prev_starts[0] % planes, prev_starts[2]])
    core_scalar = core.reshape(1).astype(jnp.int32)
    padded = jnp.zeros((SLOT, SLOT), f32).at[:nproj, :nproj].set(coupling.T)
    coupling_wide = jnp.kron(jnp.eye(atoms, dtype=f32), padded)
    across, along = stencils(planes, rows)

    steps = 4
    partial = pl.pallas_call(
        density_kernel,
        grid=(steps,),
        in_specs=[
            smem(),
            pl.BlockSpec((count, planes // steps, rows, lanes), lambda i: (0, i, 0, 0)),
        ],
        out_specs=pl.BlockSpec((planes // steps, rows, lanes), lambda i: (i, 0, 0)),
        out_shape=jax.ShapeDtypeStruct((planes, rows, lanes), f32),
        compiler_params=params(),
        name="density",
    )(occupations, orbitals)

    scratch = [
        pltpu.VMEM((atoms, square // lanes, SLOT * box, lanes), f32),
        pltpu.VMEM((slots, rows * lanes), bf16),
    ]
    own_part = pl.pallas_call(
        functools.partial(coefficient_kernel, False),
        in_specs=[smem(), smem(), vmem(), vmem()],
        out_specs=vmem(),
        out_shape=jax.ShapeDtypeStruct((count, slots), f32),
        scratch_shapes=scratch + [pltpu.VMEM((count * rows, lanes), f32)],
        compiler_params=params(),
        name="own_coefficients",
    )(own_starts, core_scalar, orbitals, projectors)

    pair = partial + swap(partial, "band", 1)
    density = pair.astype(bf16)
    mask = 2
    while mask < n_band:
        density = density.astype(f32) + swap(density, "band", mask).astype(f32)
        mask *= 2
        if mask < n_band:
            density = density.astype(bf16)
    density = density.astype(f32)
    charge = jnp.full((8, lanes), jnp.sum(density), f32)
    mask = 1
    while mask < n_space:
        charge = charge + swap(charge, "space", mask)
        mask *= 2
    mean = charge[0, :1] / (planes * rows * lanes * n_space)

    def message(part, planes_h, planes_d):
        return jnp.concatenate(
            [part, planes_h.reshape(2 * rows, lanes), planes_d.reshape(rows, lanes)], axis=0
        )

    below = around(message(own_part, hartree_prev[planes - 2 :], density[planes - 1 :]), "space", 1)

    prev_part = pl.pallas_call(
        functools.partial(coefficient_kernel, True),
        in_specs=[smem(), smem(), vmem(), vmem(), vmem()],
        out_specs=vmem(),
        out_shape=jax.ShapeDtypeStruct((count, slots), f32),
        scratch_shapes=scratch + [pltpu.VMEM((count * rows, lanes), f32)],
        compiler_params=params(),
        name="carried_coefficients",
    )(prev_starts, core_scalar, orbitals, mine, other)

    above = around(message(prev_part, hartree_prev[:2], density[:1]), "space", -1)

    acc = pl.pallas_call(
        local_kernel,
        in_specs=[smem(), smem(), hbm(), hbm(), hbm()] + [vmem()] * 8,
        out_specs=vmem(),
        out_shape=jax.ShapeDtypeStruct((count, planes, rows, lanes), f32),
        scratch_shapes=scratch
        + [
            pltpu.VMEM((count * planes * rows, lanes), f32),
            pltpu.VMEM((count, planes + 4, rows, lanes), bf16),
            pltpu.SemaphoreType.DMA((3,)),
        ],
        compiler_params=params(),
        name="local_part",
    )(
        prev_starts, core_scalar, orbitals, low, high, mine, other, prev_part, below[:count],
        coupling_wide, along, across, potential_in,
    )

    applied, potential = pl.pallas_call(
        final_kernel,
        in_specs=[smem(), smem()] + [vmem()] * 10,
        out_specs=(vmem(), vmem()),
        out_shape=(
            jax.ShapeDtypeStruct((count, planes, rows, lanes), bf16),
            jax.ShapeDtypeStruct((planes, rows, lanes), f32),
        ),
        scratch_shapes=scratch + [pltpu.VMEM((count * planes * rows, lanes), f32)],
        compiler_params=params(),
        name="final_part",
    )(
        own_starts, mean, acc, projectors, own_part, above, coupling_wide,
        density, hartree_prev, ionic_potential, below, above,
    )
    return applied, potential


def solution(mesh):
    placed = (
        P("band", "space", None, None),
        P("band"),
        P("space", None, None),
        P("space", None, None),
        P("space", None, None),
        P("space", None, None, None),
        P(),
        P(),
    )
    return jax.shard_map(
        local,
        mesh=mesh,
        in_specs=placed,
        out_specs=(P("band", "space", None, None), P("space", None, None)),
        check_vma=False,
    )
```

```python
import functools
import math

import jax
import jax.numpy as jnp
from jax import lax
from jax.experimental import pallas as pl
from jax.experimental.pallas import tpu as pltpu
from jax.sharding import PartitionSpec as P

SWEEPS = 2
LANES = 128
SLOT = 16
LIMIT = 24

screening = 0.25
four_pi = 4.0 * math.pi
f32 = jnp.float32
bf16 = jnp.bfloat16


def vmem():
    return pl.BlockSpec(memory_space=pltpu.VMEM)


def smem():
    return pl.BlockSpec(memory_space=pltpu.SMEM)


def hbm():
    return pl.BlockSpec(memory_space=pl.ANY)


NT = (((1,), (1,)), ((), ()))


def prepare_kernel(occ, field_ref, density_ref, turned_ref, first_ref, last_ref, wide_ref):
    step = pl.program_id(0)
    count, planes, rows, _ = field_ref.shape
    stride = rows + 1

    @pl.when(step == 0)
    def _():
        first_ref[...] = field_ref[:, :2]

    @pl.when(step == pl.num_programs(0) - 1)
    def _():
        last_ref[...] = field_ref[:, planes - 2 :]

    for i in range(planes):
        total = jnp.zeros((rows, LANES), f32)
        for o in range(count):
            cells = field_ref[o, i].astype(f32)
            total = total + (occ[o] * cells) * cells
            wide_ref[i, o * stride : o * stride + rows, :] = cells
        density_ref[i] = total
        turned_ref[i] = jnp.concatenate(
            [
                pltpu.roll(
                    wide_ref[i, pl.ds(r, count, stride=stride), :], (SLOT * r) % LANES, 1
                )
                for r in range(rows)
            ],
            axis=1,
        ).astype(bf16)


def shift_projectors(raw_ref, index, atom, column, rows_ref, shifted_ref):
    nproj, box, square = raw_ref.shape[1:]
    stride = box + 1
    tiles = square // LANES
    for p in range(SLOT):
        if p < nproj:
            cells = raw_ref[index, p].astype(f32)
        else:
            cells = jnp.zeros((box, square), f32)
        for t in range(tiles):
            rows_ref[t, p * stride : p * stride + box, :] = cells[:, t * LANES : (t + 1) * LANES]
    for j in range(box):
        for t in range(tiles):
            cells = rows_ref[t, pl.ds(j, SLOT, stride=stride), :].astype(bf16)
            k = j * tiles + t
            shifted_ref[atom, :, k * LANES : (k + 1) * LANES] = pltpu.roll(cells, column, 1)


def lane_group(column, height):
    lane = lax.broadcasted_iota(jnp.int32, (height, LANES), 1)
    return lax.shift_right_logical(jnp.bitwise_and(lane - column + LANES, LANES - 1), 4)


def gather_atom(turned_ref, shifted_ref, atom, offset, column, lift, boxed_ref):
    planes, count, _ = turned_ref.shape
    box = SLOT
    tiles = shifted_ref.shape[2] // (box * LANES)
    per_tile = LANES // box
    group = lane_group(column, count)
    masks = [group == r for r in range(per_tile)]
    for j in range(box):
        plane = offset + j - lift
        valid = jnp.logical_and(plane >= 0, plane < planes)
        plane = jnp.clip(plane, 0, planes - 1)
        for t in range(tiles):
            base = t * per_tile * LANES
            cells = turned_ref[plane, :, base : base + LANES]
            for r in range(1, per_tile):
                low = base + r * LANES
                cells = jnp.where(masks[r], turned_ref[plane, :, low : low + LANES], cells)
            k = j * tiles + t
            boxed_ref[:, k * LANES : (k + 1) * LANES] = jnp.where(valid, cells, jnp.zeros_like(cells))
    return lax.dot_general(boxed_ref[...], shifted_ref[atom], NT, preferred_element_type=f32)


def own_kernel(
    starts, turned_ref, proj_ref, coupling_ref,
    part_ref, shifted_ref, wide_coupling_ref, rows_ref, boxed_ref,
):
    atoms, nproj = proj_ref.shape[:2]
    for a in range(atoms):
        shift_projectors(proj_ref, a, a, starts[1, a], rows_ref.at[a % 2], shifted_ref)
    for a in range(atoms):
        part_ref[:, a * SLOT : (a + 1) * SLOT] = gather_atom(
            turned_ref, shifted_ref, a, starts[0, a], starts[1, a], 0, boxed_ref.at[a % 2]
        )
    slots = atoms * SLOT
    spread = (
        lax.broadcasted_iota(jnp.int32, (nproj, slots), 0)
        == lax.broadcasted_iota(jnp.int32, (nproj, slots), 1) % SLOT
    ).astype(f32)
    exact = dict(precision=lax.Precision.HIGHEST, preferred_element_type=f32)
    right = lax.dot_general(coupling_ref[...], spread, (((0,), (0,)), ((), ())), **exact)
    both = lax.dot_general(spread, right, (((0,), (0,)), ((), ())), **exact)
    same = (
        lax.broadcasted_iota(jnp.int32, (slots, slots), 0) // SLOT
        == lax.broadcasted_iota(jnp.int32, (slots, slots), 1) // SLOT
    )
    wide_coupling_ref[...] = jnp.where(same, both, 0.0)


def carried_kernel(
    starts, core, turned_ref, mine_ref, other_ref, hart_ref, dens_ref,
    message_ref, shifted_ref, rows_ref, boxed_ref,
):
    half = mine_ref.shape[0]
    count = turned_ref.shape[1]
    rows = hart_ref.shape[1]
    for q in range(half):
        a = core[0] * half + q
        shift_projectors(mine_ref, q, a, starts[1, a], rows_ref.at[0], shifted_ref)
        a = (1 - core[0]) * half + q
        shift_projectors(other_ref, q, a, starts[1, a], rows_ref.at[1], shifted_ref)
    for a in range(2 * half):
        message_ref[:count, a * SLOT : (a + 1) * SLOT] = gather_atom(
            turned_ref, shifted_ref, a, starts[0, a], starts[1, a],
            turned_ref.shape[0], boxed_ref.at[a % 2],
        )
    message_ref[count : count + 2 * rows] = hart_ref[:2].reshape(2 * rows, LANES)
    message_ref[count + 2 * rows :] = dens_ref[0]


def weigh(coef, coupling_ref):
    return lax.dot_general(
        coef, coupling_ref[...], (((1,), (0,)), ((), ())),
        precision=lax.Precision.HIGHEST, preferred_element_type=f32,
    ).astype(bf16)


def deposit_plane(starts, shifted_ref, weighted, plane, lift, placed_ref, wide_ref):
    atoms = shifted_ref.shape[0]
    count = weighted.shape[0]
    box = SLOT
    tiles = shifted_ref.shape[2] // (box * LANES)
    per_tile = LANES // box
    for a in range(atoms):
        group = lane_group(starts[1, a], SLOT)
        j = plane - starts[0, a] + lift
        valid = jnp.logical_and(j >= 0, j < box)
        group = jnp.where(valid, group, -1)
        j = jnp.clip(j, 0, box - 1)
        for t in range(tiles):
            low = pl.multiple_of((j * tiles + t) * LANES, LANES)
            cells = shifted_ref[a, :, pl.ds(low, LANES)]
            for r in range(per_tile):
                row = t * per_tile + r
                placed_ref[a * SLOT : (a + 1) * SLOT, row * LANES : (row + 1) * LANES] = jnp.where(
                    group == r, cells, jnp.zeros_like(cells)
                )
    update = jnp.dot(weighted, placed_ref[...], preferred_element_type=f32)
    rows = tiles * per_tile
    for r in range(rows):
        wide_ref[pl.ds(r, count, stride=rows + 1), :] = pltpu.roll(
            update[:, r * LANES : (r + 1) * LANES], (-SLOT * r) % LANES, 1
        )


def local_kernel(
    starts, field_ref, low_ref, high_ref, shifted_ref, message_ref, below_ref,
    coupling_ref, pot_ref, acc_ref, placed_ref, wide_ref,
):
    count, planes, rows, _ = field_ref.shape
    weighted = weigh(message_ref[:count] + below_ref[:count], coupling_ref)

    def one(o, _):
        cells = (
            [low_ref[o, i].astype(f32) for i in range(2)]
            + [field_ref[o, i].astype(f32) for i in range(planes)]
            + [high_ref[o, i].astype(f32) for i in range(2)]
        )
        for i in range(planes):
            c = cells[i + 2]
            near = cells[i + 1] + cells[i + 3]
            near = near + pltpu.roll(c, 1, 0) + pltpu.roll(c, rows - 1, 0)
            near = near + pltpu.roll(c, 1, 1) + pltpu.roll(c, LANES - 1, 1)
            far = cells[i] + cells[i + 4]
            far = far + pltpu.roll(c, 2, 0) + pltpu.roll(c, rows - 2, 0)
            far = far + pltpu.roll(c, 2, 1) + pltpu.roll(c, LANES - 2, 1)
            acc_ref[o, i] = (
                (pot_ref[i] + 3.75) * c - (2.0 / 3.0) * near + (1.0 / 24.0) * far
            )
        return 0

    lax.fori_loop(0, count, one, 0)

    def two(plane, _):
        deposit_plane(starts, shifted_ref, weighted, plane, planes, placed_ref, wide_ref)
        for o in range(count):
            low = o * (rows + 1)
            acc_ref[o, plane] += wide_ref[low : low + rows, :]
        return 0

    lax.fori_loop(0, planes, two, 0)


def final_kernel(
    starts, acc_ref, shifted_ref, part_ref, above_ref, coupling_ref,
    dens_ref, hart_ref, ionic_ref, below_ref, charge_ref,
    out_ref, pot_ref, placed_ref, wide_ref, done_ref, sems, *, cells_total,
):
    count, planes, rows, _ = done_ref.shape
    weighted = weigh(part_ref[...] + above_ref[:count], coupling_ref)
    groups = sems.shape[0]
    size = planes // groups
    copies = []
    for group in range(groups):
        def two(i, _):
            plane = group * size + i
            deposit_plane(starts, shifted_ref, weighted, plane, 0, placed_ref, wide_ref)
            for o in range(count):
                low = o * (rows + 1)
                done_ref[o, plane] = (acc_ref[o, plane] + wide_ref[low : low + rows, :]).astype(bf16)
            return 0

        lax.fori_loop(0, size, two, 0)
        part = pl.ds(group * size, size)
        copies.append(
            pltpu.make_async_copy(done_ref.at[:, part], out_ref.at[:, part], sems.at[group])
        )
        copies[-1].start()

    field = jnp.concatenate(
        [
            below_ref[count : count + 2 * rows].reshape(2, rows, LANES),
            hart_ref[...],
            above_ref[count : count + 2 * rows].reshape(2, rows, LANES),
        ],
        axis=0,
    )
    dens = jnp.concatenate(
        [
            below_ref[count + 2 * rows :].reshape(1, rows, LANES),
            dens_ref[...],
            above_ref[count + 2 * rows :].reshape(1, rows, LANES),
        ],
        axis=0,
    )
    source = four_pi * dens
    scale = 1.0 / (6.0 + screening)

    def relax(h, s):
        inner = h[1:-1]
        size = inner.shape
        flat = inner.reshape(size[0] * rows, LANES)
        across = pltpu.roll(flat, 1, 1) + pltpu.roll(flat, LANES - 1, 1)
        total = h[2:] + h[:-2] + across.reshape(size)
        total = total + pltpu.roll(inner, 1, 1) + pltpu.roll(inner, rows - 1, 1)
        return (total + s) * scale

    once = relax(field, source)
    twice = relax(once, source[1:-1])
    shift = charge_ref[0:1, 0:1] * (four_pi * scale * (1.0 + 6.0 * scale) / cells_total)
    third = (3.0 / math.pi) * dens_ref[...]
    root = jnp.exp(jnp.log(jnp.maximum(third, 1e-37)) * (1.0 / 3.0))
    root = (2.0 * root + third / jnp.maximum(root * root, 1e-30)) * (1.0 / 3.0)
    root = jnp.where(third > 0.0, root, 0.0)
    pot_ref[...] = ionic_ref[...] + twice - shift[None] - root
    for copy in copies:
        copy.wait()


def around(block, axis, distance):
    count = lax.axis_size(axis)
    return lax.ppermute(block, axis, [(i, (i + distance) % count) for i in range(count)])


def swap(block, axis, mask):
    return lax.ppermute(block, axis, [(i, i ^ mask) for i in range(lax.axis_size(axis))])


def local(
    orbitals, occupations, potential_in, ionic_potential, hartree_prev, projectors, box_start, coupling
):
    count, planes, rows, lanes = orbitals.shape
    atoms, nproj, box, square = projectors.shape
    n_space = lax.axis_size("space")
    n_band = lax.axis_size("band")
    domain = lax.axis_index("space")
    core = lax.axis_index("band") % 2
    half = atoms // 2
    slots = atoms * SLOT
    cells = planes * rows * lanes
    params = pltpu.CompilerParams(vmem_limit_bytes=LIMIT << 20)

    def call(kernel, name, work, **kwargs):
        cost = pl.CostEstimate(flops=work * 500000, bytes_accessed=work * 1000000, transcendentals=0)
        return pl.pallas_call(kernel, name=name, compiler_params=params, cost_estimate=cost, **kwargs)

    mine = around(lax.dynamic_slice_in_dim(projectors, core * half, half, 0), "space", 1)
    other = swap(mine, "band", 1)

    behind = (domain + n_space - 1) % n_space
    own_starts = lax.dynamic_slice_in_dim(box_start, domain * atoms, atoms, 1)
    own_starts = jnp.stack([own_starts[0] % planes, own_starts[2]])
    prev_starts = lax.dynamic_slice_in_dim(box_start, behind * atoms, atoms, 1)
    prev_starts = jnp.stack([prev_starts[0] % planes, prev_starts[2]])
    core_scalar = core.reshape(1).astype(jnp.int32)

    steps = 4
    step = planes // steps
    stride = rows + 1
    partial, turned, first, last = call(
        prepare_kernel, "prepare", 2,
        grid=(steps,),
        in_specs=[smem(), pl.BlockSpec((count, step, rows, lanes), lambda i: (0, i, 0, 0))],
        out_specs=(
            pl.BlockSpec((step, rows, lanes), lambda i: (i, 0, 0)),
            pl.BlockSpec((step, count, rows * lanes), lambda i: (i, 0, 0)),
            pl.BlockSpec((count, 2, rows, lanes), lambda i: (0, 0, 0, 0)),
            pl.BlockSpec((count, 2, rows, lanes), lambda i: (0, 0, 0, 0)),
        ),
        out_shape=(
            jax.ShapeDtypeStruct((planes, rows, lanes), f32),
            jax.ShapeDtypeStruct((planes, count, rows * lanes), bf16),
            jax.ShapeDtypeStruct((count, 2, rows, lanes), bf16),
            jax.ShapeDtypeStruct((count, 2, rows, lanes), bf16),
        ),
        scratch_shapes=[pltpu.VMEM((step, count * stride, lanes), f32)],
    )(occupations, orbitals)
    low = around(last, "space", 1)
    high = around(first, "space", -1)

    shifted_shape = jax.ShapeDtypeStruct((atoms, SLOT, box * square), bf16)
    gather_scratch = [
        pltpu.VMEM((2, square // lanes, SLOT * (box + 1), lanes), f32),
        pltpu.VMEM((2, count, box * square), bf16),
    ]
    own_part, own_shifted, wide_coupling = call(
        own_kernel, "own_part", 4,
        in_specs=[smem()] + [vmem()] * 3,
        out_specs=(vmem(), vmem(), vmem()),
        out_shape=(
            jax.ShapeDtypeStruct((count, slots), f32),
            shifted_shape,
            jax.ShapeDtypeStruct((slots, slots), f32),
        ),
        scratch_shapes=gather_scratch,
    )(own_starts, turned, projectors, coupling)

    pair = partial + swap(partial, "band", 1)
    density = pair.astype(bf16)
    mask = 2
    while mask < n_band:
        density = density.astype(f32) + swap(density, "band", mask).astype(f32)
        mask *= 2
        if mask < n_band:
            density = density.astype(bf16)
    density = density.astype(f32)
    charge = jnp.full((8, lanes), jnp.sum(density), f32)
    mask = 1
    while mask < n_space:
        charge = charge + swap(charge, "space", mask)
        mask *= 2

    below = around(
        jnp.concatenate(
            [
                own_part,
                hartree_prev[planes - 2 :].reshape(2 * rows, lanes),
                density[planes - 1],
            ],
            axis=0,
        ),
        "space",
        1,
    )

    message, prev_shifted = call(
        carried_kernel, "carried_part", 4,
        in_specs=[smem(), smem()] + [vmem()] * 5,
        out_specs=(vmem(), vmem()),
        out_shape=(jax.ShapeDtypeStruct((count + 3 * rows, slots), f32), shifted_shape),
        scratch_shapes=gather_scratch,
    )(prev_starts, core_scalar, turned, mine, other, hartree_prev, density)

    above = around(message, "space", -1)

    deposit_scratch = [
        pltpu.VMEM((slots, rows * lanes), bf16),
        pltpu.VMEM((count * stride, lanes), f32),
    ]
    acc = call(
        local_kernel, "local_part", 6,
        in_specs=[smem()] + [vmem()] * 8,
        out_specs=vmem(),
        out_shape=jax.ShapeDtypeStruct((count, planes, rows, lanes), f32),
        scratch_shapes=deposit_scratch,
    )(
        prev_starts, orbitals, low, high, prev_shifted, message, below, wide_coupling, potential_in
    )

    applied, potential = call(
        functools.partial(final_kernel, cells_total=float(cells * n_space)), "final_part", 4,
        in_specs=[smem()] + [vmem()] * 10,
        out_specs=(hbm(), vmem()),
        out_shape=(
            jax.ShapeDtypeStruct((count, planes, rows, lanes), bf16),
            jax.ShapeDtypeStruct((planes, rows, lanes), f32),
        ),
        scratch_shapes=deposit_scratch
        + [
            pltpu.VMEM((count, planes, rows, lanes), bf16),
            pltpu.SemaphoreType.DMA((4,)),
        ],
    )(
        own_starts, acc, own_shifted, own_part, above, wide_coupling,
        density, hartree_prev, ionic_potential, below, charge,
    )
    return applied, potential


def solution(mesh):
    placed = (
        P("band", "space", None, None),
        P("band"),
        P("space", None, None),
        P("space", None, None),
        P("space", None, None),
        P("space", None, None, None),
        P(),
        P(),
    )
    return jax.shard_map(
        local,
        mesh=mesh,
        in_specs=placed,
        out_specs=(P("band", "space", None, None), P("space", None, None)),
        check_vma=False,
    )
```

```python
import functools
import math

import jax
import jax.numpy as jnp
from jax import lax
from jax.experimental import pallas as pl
from jax.experimental.pallas import tpu as pltpu
from jax.sharding import PartitionSpec as P


LANES = 128
SLOT = 16
LIMIT = 24

screening = 0.25
four_pi = 4.0 * math.pi
f32 = jnp.float32
bf16 = jnp.bfloat16


def vmem():
    return pl.BlockSpec(memory_space=pltpu.VMEM)


def smem():
    return pl.BlockSpec(memory_space=pltpu.SMEM)


def high_hbm():
    return pl.BlockSpec(memory_space=pltpu.HBM)


def hbm():
    return pl.BlockSpec(memory_space=pl.ANY)


NT = (((1,), (1,)), ((), ()))


def start_of(starts, atom, atoms, planes, carried):
    domain = lax.axis_index("space")
    if carried:
        count = lax.axis_size("space")
        domain = lax.rem(domain + (count - 1), count)
    index = domain * atoms + atom
    return lax.rem(starts[0, index], planes), starts[2, index]


def pick_kernel(proj_ref, out_ref, sem):
    half = out_ref.shape[0]
    core = lax.rem(lax.axis_index("band"), 2)
    copy = pltpu.make_async_copy(proj_ref.at[pl.ds(core * half, half)], out_ref, sem)
    copy.start()
    copy.wait()


def prepare_kernel(
    occ, field_hbm, density_ref, turned_ref, first_ref, last_ref, field_ref, wide_ref, sems
):
    count, planes, rows, _ = field_ref.shape
    stride = rows + 1
    groups = sems.shape[0]
    size = planes // groups
    copies = [
        pltpu.make_async_copy(
            field_hbm.at[:, pl.ds(g * size, size)], field_ref.at[:, pl.ds(g * size, size)], sems.at[g]
        )
        for g in range(groups)
    ]
    for copy in copies:
        copy.start()
    for g in range(groups):
        copies[g].wait()

        def one(i):
            plane = g * size + i
            total = jnp.zeros((rows, LANES), f32)
            for o in range(count):
                cells = field_ref[o, plane].astype(f32)
                total = total + (occ[o] * cells) * cells
                wide_ref[i % 2, o * stride : o * stride + rows, :] = cells
            density_ref[plane] = total
            turned_ref[plane] = jnp.concatenate(
                [
                    pltpu.roll(
                        wide_ref[i % 2, pl.ds(r, count, stride=stride), :], (SLOT * r) % LANES, 1
                    )
                    for r in range(rows)
                ],
                axis=1,
            ).astype(bf16)

        for i in range(size):
            one(i)
    first_ref[...] = field_ref[:, :2]
    last_ref[...] = field_ref[:, planes - 2 :]


def shift_projectors(raw_ref, index, atom, column, rows_ref, shifted_ref):
    nproj, box, square = raw_ref.shape[1:]
    stride = box + 1
    tiles = square // LANES
    for p in range(SLOT):
        if p < nproj:
            cells = raw_ref[index, p].astype(f32)
        else:
            cells = jnp.zeros((box, square), f32)
        for t in range(tiles):
            rows_ref[t, p * stride : p * stride + box, :] = cells[:, t * LANES : (t + 1) * LANES]
    for j in range(box):
        for t in range(tiles):
            cells = rows_ref[t, pl.ds(j, SLOT, stride=stride), :].astype(bf16)
            k = j * tiles + t
            shifted_ref[atom, :, k * LANES : (k + 1) * LANES] = pltpu.roll(cells, column, 1)
    shifted_ref[atom, :, box * square :] = jnp.zeros((SLOT, square), bf16)


def lane_group(column, height):
    lane = lax.broadcasted_iota(jnp.int32, (height, LANES), 1)
    return lax.shift_right_logical(jnp.bitwise_and(lane - column + LANES, LANES - 1), 4)


def gather_atom(turned_ref, shifted_ref, atom, offset, column, lift, boxed_ref):
    planes, count, _ = turned_ref.shape
    box = SLOT
    tiles = boxed_ref.shape[1] // (box * LANES)
    per_tile = LANES // box
    group = lane_group(column, count)
    masks = [group == r for r in range(per_tile)]
    for j in range(box):
        plane = offset + j - lift
        valid = jnp.logical_and(plane >= 0, plane < planes)
        plane = jnp.clip(plane, 0, planes - 1)
        for t in range(tiles):
            base = t * per_tile * LANES
            cells = turned_ref[plane, :, base : base + LANES]
            for r in range(1, per_tile):
                low = base + r * LANES
                cells = jnp.where(masks[r], turned_ref[plane, :, low : low + LANES], cells)
            k = j * tiles + t
            boxed_ref[:, k * LANES : (k + 1) * LANES] = jnp.where(valid, cells, jnp.zeros_like(cells))
    shifted = shifted_ref[atom, :, : boxed_ref.shape[1]]
    return lax.dot_general(boxed_ref[...], shifted, NT, preferred_element_type=f32)


def own_kernel(
    starts, turned_ref, proj_ref, coupling_ref, partial_ref, partner_ref,
    part_ref, shifted_ref, wide_coupling_ref, pair_ref, rows_ref, boxed_ref,
):
    atoms, nproj = proj_ref.shape[:2]
    pair_ref[...] = (partial_ref[...] + partner_ref[...]).astype(pair_ref.dtype)
    planes = turned_ref.shape[0]
    for a in range(atoms):
        offset, column = start_of(starts, a, atoms, planes, False)
        shift_projectors(proj_ref, a, a, column, rows_ref.at[a % 2], shifted_ref)
    for a in range(atoms):
        offset, column = start_of(starts, a, atoms, planes, False)
        part_ref[:, a * SLOT : (a + 1) * SLOT] = gather_atom(
            turned_ref, shifted_ref, a, offset, column, 0, boxed_ref.at[a % 2]
        )
    slots = atoms * SLOT
    spread = (
        lax.broadcasted_iota(jnp.int32, (nproj, slots), 0)
        == lax.broadcasted_iota(jnp.int32, (nproj, slots), 1) % SLOT
    ).astype(f32)
    exact = dict(precision=lax.Precision.HIGHEST, preferred_element_type=f32)
    right = lax.dot_general(coupling_ref[...], spread, (((0,), (0,)), ((), ())), **exact)
    both = lax.dot_general(spread, right, (((0,), (0,)), ((), ())), **exact)
    same = (
        lax.broadcasted_iota(jnp.int32, (slots, slots), 0) // SLOT
        == lax.broadcasted_iota(jnp.int32, (slots, slots), 1) // SLOT
    )
    wide_coupling_ref[...] = jnp.where(same, both, 0.0)


def carried_kernel(
    starts, turned_ref, mine_ref, other_ref, hart_ref, dens_ref,
    message_ref, shifted_ref, rows_ref, boxed_ref,
):
    half = mine_ref.shape[0]
    planes, count, _ = turned_ref.shape
    rows = hart_ref.shape[1]
    core = lax.rem(lax.axis_index("band"), 2)
    for q in range(half):
        a = core * half + q
        offset, column = start_of(starts, a, 2 * half, planes, True)
        shift_projectors(mine_ref, q, a, column, rows_ref.at[0], shifted_ref)
        a = (1 - core) * half + q
        offset, column = start_of(starts, a, 2 * half, planes, True)
        shift_projectors(other_ref, q, a, column, rows_ref.at[1], shifted_ref)
    for a in range(2 * half):
        offset, column = start_of(starts, a, 2 * half, planes, True)
        message_ref[:count, a * SLOT : (a + 1) * SLOT] = gather_atom(
            turned_ref, shifted_ref, a, offset, column, planes, boxed_ref.at[a % 2]
        )
    message_ref[count : count + 2 * rows] = hart_ref[:2].reshape(2 * rows, LANES)
    message_ref[count + 2 * rows :] = dens_ref[0]


def weigh(coef, coupling_ref):
    return lax.dot_general(
        coef, coupling_ref[...], (((1,), (0,)), ((), ())),
        precision=lax.Precision.HIGHEST, preferred_element_type=f32,
    ).astype(bf16)


def lane_masks(starts, planes, carried, masks_ref):
    atoms, per_tile = masks_ref.shape[:2]
    for a in range(atoms):
        group = lane_group(start_of(starts, a, atoms, planes, carried)[1], SLOT)
        for r in range(per_tile):
            masks_ref[a, r] = jnp.where(group == r, 1.0, 0.0).astype(bf16)


def deposit_plane(starts, shifted_ref, masks_ref, weighted, plane, planes, carried, wide_ref):
    atoms, per_tile = masks_ref.shape[:2]
    count = weighted.shape[0]
    box = SLOT
    tiles = shifted_ref.shape[2] // ((box + 1) * LANES)
    rows = tiles * per_tile
    places = []
    for a in range(atoms):
        j = plane - start_of(starts, a, atoms, planes, carried)[0]
        if carried:
            j = j + planes
        places.append(jnp.where(jnp.logical_and(j >= 0, j < box), j, box) * (tiles * LANES))
    for t in range(tiles):
        cells = [
            shifted_ref[a, :, pl.ds(pl.multiple_of(places[a] + t * LANES, LANES), LANES)]
            for a in range(atoms)
        ]
        for r in range(per_tile):
            placed = jnp.concatenate([cells[a] * masks_ref[a, r] for a in range(atoms)], axis=0)
            update = jnp.dot(weighted, placed, preferred_element_type=f32)
            row = t * per_tile + r
            wide_ref[pl.ds(row, count, stride=rows + 1), :] = pltpu.roll(
                update, (-SLOT * row) % LANES, 1
            )


def pad_rows(padded_ref, index, cells):
    rows = cells.shape[0]
    base = index * (rows + 8)
    padded_ref[base + 2 : base + 2 + rows, :] = cells
    padded_ref[base : base + 2, :] = cells[rows - 2 :]
    padded_ref[base + 2 + rows : base + 4 + rows, :] = cells[:2]


def stencil_plane(padded_ref, index, below2, below1, c, above1, above2, potential):
    rows = c.shape[0]
    base = index * (rows + 8)
    near = below1 + above1
    near = near + padded_ref[base + 1 : base + 1 + rows, :] + padded_ref[base + 3 : base + 3 + rows, :]
    near = near + pltpu.roll(c, 1, 1) + pltpu.roll(c, LANES - 1, 1)
    far = below2 + above2
    far = far + padded_ref[base : base + rows, :] + padded_ref[base + 4 : base + 4 + rows, :]
    far = far + pltpu.roll(c, 2, 1) + pltpu.roll(c, LANES - 2, 1)
    return (potential + 3.75) * c - (2.0 / 3.0) * near + (1.0 / 24.0) * far


def inner_kernel(field_ref, pot_ref, acc_ref, padded_ref):
    count, planes, _, _ = field_ref.shape

    def one(o, _):
        cells = [field_ref[o, i].astype(f32) for i in range(planes)]
        for i in range(2, planes - 2):
            pad_rows(padded_ref, i, cells[i])
            acc_ref[o, i] = stencil_plane(padded_ref, i, *cells[i - 2 : i + 3], pot_ref[i])
        return 0

    lax.fori_loop(0, count, one, 0)


def add_kernel(one_ref, other_ref, out_ref):
    out_ref[...] = one_ref[...] + other_ref[...]


def shift_kernel(cells, pot_ref, charge_ref, out_ref):
    scale = 1.0 / (6.0 + screening)
    shift = charge_ref[0:1, 0:1] * (four_pi * scale * (1.0 + 6.0 * scale) / cells)
    out_ref[...] = pot_ref[...] - shift[None]


def join_kernel(pair_ref, partner_ref, part_ref, hart_ref, density_ref, charge_ref, message_ref):
    planes, rows, _ = density_ref.shape
    count = part_ref.shape[0]
    density = pair_ref[...].astype(f32) + partner_ref[...].astype(f32)
    density_ref[...] = density
    charge_ref[...] = jnp.full(charge_ref.shape, jnp.sum(density), f32)
    message_ref[:count] = part_ref[...]
    message_ref[count : count + 2 * rows] = hart_ref[planes - 2 :].reshape(2 * rows, LANES)
    message_ref[count + 2 * rows :] = density[planes - 1]


def local_kernel(
    starts, inner_ref, field_ref, low_ref, high_ref, shifted_ref, message_ref, below_ref,
    coupling_ref, pot_ref, acc_ref, masks_ref, wide_ref, padded_ref,
):
    count, planes, rows, _ = field_ref.shape
    lane_masks(starts, planes, True, masks_ref)
    weighted = weigh(message_ref[:count] + below_ref[:count], coupling_ref)

    def one(o, _):
        cells = {i: field_ref[o, i].astype(f32) for i in (0, 1, 2, 3)}
        cells.update({i: field_ref[o, i].astype(f32) for i in range(planes - 4, planes)})
        for i in range(2):
            cells[i - 2] = low_ref[o, i].astype(f32)
            cells[planes + i] = high_ref[o, i].astype(f32)
        for k, i in enumerate((0, 1, planes - 2, planes - 1)):
            pad_rows(padded_ref, k, cells[i])
            acc_ref[o, i] = stencil_plane(
                padded_ref, k, *[cells[i + d] for d in range(-2, 3)], pot_ref[i]
            )
        return 0

    lax.fori_loop(0, count, one, 0)

    def two(pair, _):
        for half in range(2):
            plane = 2 * pair + half
            deposit_plane(
                starts, shifted_ref, masks_ref, weighted, plane, planes, True, wide_ref.at[half]
            )
            for o in range(count):
                low = o * (rows + 1)
                acc_ref[o, plane] += wide_ref[half, low : low + rows, :]
        return 0

    lax.fori_loop(0, planes // 2, two, 0)


def final_kernel(
    starts, acc_ref, shifted_ref, part_ref, above_ref, coupling_ref,
    dens_ref, hart_ref, ionic_ref, below_ref,
    out_ref, pot_ref, masks_ref, wide_ref, done_ref, sems,
):
    count, planes, rows, _ = done_ref.shape
    lane_masks(starts, planes, False, masks_ref)
    weighted = weigh(part_ref[...] + above_ref[:count], coupling_ref)
    groups = sems.shape[0]
    size = planes // groups
    copies = []
    for group in range(groups):
        def two(pair, _):
            for half in range(2):
                plane = group * size + 2 * pair + half
                deposit_plane(
                    starts, shifted_ref, masks_ref, weighted, plane, planes, False, wide_ref.at[half]
                )
                for o in range(count):
                    low = o * (rows + 1)
                    done_ref[o, plane] = (
                        acc_ref[o, plane] + wide_ref[half, low : low + rows, :]
                    ).astype(bf16)
            return 0

        lax.fori_loop(0, size // 2, two, 0)
        part = pl.ds(group * size, size)
        copies.append(
            pltpu.make_async_copy(done_ref.at[:, part], out_ref.at[:, part], sems.at[group])
        )
        copies[-1].start()

    field = jnp.concatenate(
        [
            below_ref[count : count + 2 * rows].reshape(2, rows, LANES),
            hart_ref[...],
            above_ref[count : count + 2 * rows].reshape(2, rows, LANES),
        ],
        axis=0,
    )
    dens = jnp.concatenate(
        [
            below_ref[count + 2 * rows :].reshape(1, rows, LANES),
            dens_ref[...],
            above_ref[count + 2 * rows :].reshape(1, rows, LANES),
        ],
        axis=0,
    )
    source = four_pi * dens
    scale = 1.0 / (6.0 + screening)

    def relax(h, s):
        inner = h[1:-1]
        size = inner.shape
        flat = inner.reshape(size[0] * rows, LANES)
        across = pltpu.roll(flat, 1, 1) + pltpu.roll(flat, LANES - 1, 1)
        total = h[2:] + h[:-2] + across.reshape(size)
        total = total + pltpu.roll(inner, 1, 1) + pltpu.roll(inner, rows - 1, 1)
        return (total + s) * scale

    once = relax(field, source)
    twice = relax(once, source[1:-1])
    third = (3.0 / math.pi) * dens_ref[...]
    root = jnp.exp(jnp.log(jnp.maximum(third, 1e-37)) * (1.0 / 3.0))
    root = (2.0 * root + third / jnp.maximum(root * root, 1e-30)) * (1.0 / 3.0)
    root = jnp.where(third > 0.0, root, 0.0)
    pot_ref[...] = ionic_ref[...] + twice - root
    for copy in copies:
        copy.wait()


def around(block, axis, distance):
    count = lax.axis_size(axis)
    return lax.ppermute(block, axis, [(i, (i + distance) % count) for i in range(count)])


def swap(block, axis, mask):
    return lax.ppermute(block, axis, [(i, i ^ mask) for i in range(lax.axis_size(axis))])


def local(
    orbitals, occupations, potential_in, ionic_potential, hartree_prev, projectors, box_start, coupling
):
    count, planes, rows, lanes = orbitals.shape
    atoms, nproj, box, square = projectors.shape
    n_space = lax.axis_size("space")
    n_band = lax.axis_size("band")
    half = atoms // 2
    slots = atoms * SLOT
    cells = planes * rows * lanes
    params = pltpu.CompilerParams(vmem_limit_bytes=LIMIT << 20)

    def call(kernel, work, **kwargs):
        cost = pl.CostEstimate(flops=work * 500000, bytes_accessed=work * 1000000, transcendentals=0)
        return pl.pallas_call(kernel, compiler_params=params, cost_estimate=cost, **kwargs)

    picked = call(
        pick_kernel, 1,
        in_specs=[high_hbm()],
        out_specs=vmem(),
        out_shape=jax.ShapeDtypeStruct((half, nproj, box, square), projectors.dtype),
        scratch_shapes=[pltpu.SemaphoreType.DMA],
    )(projectors)
    mine = around(picked, "space", 1)
    other = swap(mine, "band", 1)

    groups = 4
    stride = rows + 1
    partial, turned, first, last = call(
        prepare_kernel, 2,
        in_specs=[smem(), high_hbm()],
        out_specs=(vmem(),) * 4,
        out_shape=(
            jax.ShapeDtypeStruct((planes, rows, lanes), f32),
            jax.ShapeDtypeStruct((planes, count, rows * lanes), bf16),
            jax.ShapeDtypeStruct((count, 2, rows, lanes), bf16),
            jax.ShapeDtypeStruct((count, 2, rows, lanes), bf16),
        ),
        scratch_shapes=[
            pltpu.VMEM((count, planes, rows, lanes), bf16),
            pltpu.VMEM((2, count * stride, lanes), f32),
            pltpu.SemaphoreType.DMA((groups,)),
        ],
    )(occupations, orbitals)
    low = around(last, "space", 1)
    high = around(first, "space", -1)

    shifted_shape = jax.ShapeDtypeStruct((atoms, SLOT, (box + 1) * square), bf16)
    gather_scratch = [
        pltpu.VMEM((2, square // lanes, SLOT * (box + 1), lanes), f32),
        pltpu.VMEM((2, count, box * square), bf16),
    ]
    own_part, own_shifted, wide_coupling, pair = call(
        own_kernel, 4,
        in_specs=[smem()] + [vmem()] * 5,
        out_specs=(vmem(),) * 4,
        out_shape=(
            jax.ShapeDtypeStruct((count, slots), f32),
            shifted_shape,
            jax.ShapeDtypeStruct((slots, slots), f32),
            jax.ShapeDtypeStruct((planes, rows, lanes), bf16),
        ),
        scratch_shapes=gather_scratch,
    )(box_start, turned, projectors, coupling, partial, swap(partial, "band", 1))

    inner = call(
        inner_kernel, 3,
        in_specs=[vmem(), vmem()],
        out_specs=vmem(),
        out_shape=jax.ShapeDtypeStruct((count, planes, rows, lanes), f32),
        scratch_shapes=[pltpu.VMEM((planes * (rows + 8), lanes), f32)],
    )(orbitals, potential_in)

    mask = 2
    while 2 * mask < n_band:
        pair = (pair.astype(f32) + swap(pair, "band", mask).astype(f32)).astype(bf16)
        mask *= 2
    message_shape = jax.ShapeDtypeStruct((count + 3 * rows, lanes), f32)
    density, charge, message = call(
        join_kernel, 1,
        in_specs=[vmem()] * 4,
        out_specs=(vmem(),) * 3,
        out_shape=(
            jax.ShapeDtypeStruct((planes, rows, lanes), f32),
            jax.ShapeDtypeStruct((8, lanes), f32),
            message_shape,
        ),
    )(pair, swap(pair, "band", mask), own_part, hartree_prev)
    below = around(message, "space", 1)
    mask = 1
    while mask < n_space:
        charge = call(
            add_kernel, 1,
            in_specs=[vmem(), vmem()],
            out_specs=vmem(),
            out_shape=jax.ShapeDtypeStruct((8, lanes), f32),
        )(charge, swap(charge, "space", mask))
        mask *= 2

    message, prev_shifted = call(
        carried_kernel, 4,
        in_specs=[smem()] + [vmem()] * 5,
        out_specs=(vmem(), vmem()),
        out_shape=(message_shape, shifted_shape),
        scratch_shapes=gather_scratch,
    )(box_start, turned, mine, other, hartree_prev, density)

    above = around(message, "space", -1)

    deposit_scratch = [
        pltpu.VMEM((atoms, lanes // SLOT, SLOT, lanes), bf16),
        pltpu.VMEM((2, count * stride, lanes), f32),
    ]
    acc = call(
        local_kernel, 4,
        in_specs=[smem()] + [vmem()] * 9,
        out_specs=vmem(),
        out_shape=jax.ShapeDtypeStruct((count, planes, rows, lanes), f32),
        scratch_shapes=deposit_scratch + [pltpu.VMEM((4 * (rows + 8), lanes), f32)],
        input_output_aliases={1: 0},
    )(
        box_start, inner, orbitals, low, high, prev_shifted, message, below, wide_coupling,
        potential_in,
    )

    applied, potential = call(
        final_kernel, 4,
        in_specs=[smem()] + [vmem()] * 9,
        out_specs=(hbm(), vmem()),
        out_shape=(
            jax.ShapeDtypeStruct((count, planes, rows, lanes), bf16),
            jax.ShapeDtypeStruct((planes, rows, lanes), f32),
        ),
        scratch_shapes=deposit_scratch
        + [
            pltpu.VMEM((count, planes, rows, lanes), bf16),
            pltpu.SemaphoreType.DMA((4,)),
        ],
    )(
        box_start, acc, own_shifted, own_part, above, wide_coupling,
        density, hartree_prev, ionic_potential, below,
    )
    potential = call(
        functools.partial(shift_kernel, float(cells * n_space)), 1,
        in_specs=[vmem(), vmem()],
        out_specs=vmem(),
        out_shape=jax.ShapeDtypeStruct((planes, rows, lanes), f32),
    )(potential, charge)
    return applied, potential


def solution(mesh):
    placed = (
        P("band", "space", None, None),
        P("band"),
        P("space", None, None),
        P("space", None, None),
        P("space", None, None),
        P("space", None, None, None),
        P(),
        P(),
    )

    return jax.shard_map(
        local,
        mesh=mesh,
        in_specs=placed,
        out_specs=(P("band", "space", None, None), P("space", None, None)),
        check_vma=False,
    )
```

```python
import functools
import math

import jax
import jax.numpy as jnp
from jax import lax
from jax.experimental import pallas as pl
from jax.experimental.pallas import tpu as pltpu
from jax.sharding import PartitionSpec as P


LANES = 128
SLOT = 16
LIMIT = 24

screening = 0.25
four_pi = 4.0 * math.pi
f32 = jnp.float32
bf16 = jnp.bfloat16


def vmem():
    return pl.BlockSpec(memory_space=pltpu.VMEM)


def smem():
    return pl.BlockSpec(memory_space=pltpu.SMEM)


def high_hbm():
    return pl.BlockSpec(memory_space=pltpu.HBM)


def hbm():
    return pl.BlockSpec(memory_space=pl.ANY)


NT = (((1,), (1,)), ((), ()))


def start_of(starts, atom, atoms, planes, carried):
    domain = lax.axis_index("space")
    if carried:
        count = lax.axis_size("space")
        domain = lax.rem(domain + (count - 1), count)
    index = domain * atoms + atom
    return lax.rem(starts[0, index], planes), starts[2, index]


def pick_kernel(proj_ref, out_ref, sem):
    half = out_ref.shape[0]
    core = lax.rem(lax.axis_index("band"), 2)
    copy = pltpu.make_async_copy(proj_ref.at[pl.ds(core * half, half)], out_ref, sem)
    copy.start()
    copy.wait()


def prepare_kernel(
    occ, field_hbm, density_ref, turned_ref, first_ref, last_ref, field_ref, wide_ref, sems
):
    count, planes, rows, _ = field_ref.shape
    stride = rows + 1
    groups = sems.shape[0]
    size = planes // groups
    copies = [
        pltpu.make_async_copy(
            field_hbm.at[:, pl.ds(g * size, size)], field_ref.at[:, pl.ds(g * size, size)], sems.at[g]
        )
        for g in range(groups)
    ]
    for copy in copies:
        copy.start()
    for g in range(groups):
        copies[g].wait()

        def one(i):
            plane = g * size + i
            total = jnp.zeros((rows, LANES), f32)
            for o in range(count):
                cells = field_ref[o, plane].astype(f32)
                total = total + (occ[o] * cells) * cells
                wide_ref[i % 2, o * stride : o * stride + rows, :] = cells
            density_ref[plane] = total
            turned_ref[plane] = jnp.concatenate(
                [
                    pltpu.roll(
                        wide_ref[i % 2, pl.ds(r, count, stride=stride), :], (SLOT * r) % LANES, 1
                    )
                    for r in range(rows)
                ],
                axis=1,
            ).astype(bf16)

        for i in range(size):
            one(i)
    first_ref[...] = field_ref[:, :2]
    last_ref[...] = field_ref[:, planes - 2 :]


def shift_projectors(raw_ref, index, atom, column, rows_ref, shifted_ref):
    nproj, box, square = raw_ref.shape[1:]
    stride = box + 1
    tiles = square // LANES
    for p in range(SLOT):
        if p < nproj:
            cells = raw_ref[index, p].astype(f32)
        else:
            cells = jnp.zeros((box, square), f32)
        for t in range(tiles):
            rows_ref[t, p * stride : p * stride + box, :] = cells[:, t * LANES : (t + 1) * LANES]
    for j in range(box):
        for t in range(tiles):
            cells = rows_ref[t, pl.ds(j, SLOT, stride=stride), :].astype(bf16)
            k = j * tiles + t
            shifted_ref[atom, :, k * LANES : (k + 1) * LANES] = pltpu.roll(cells, column, 1)
    shifted_ref[atom, :, box * square :] = jnp.zeros((SLOT, square), bf16)


def lane_group(column, height):
    lane = lax.broadcasted_iota(jnp.int32, (height, LANES), 1)
    return lax.shift_right_logical(jnp.bitwise_and(lane - column + LANES, LANES - 1), 4)


def gather_atom(turned_ref, shifted_ref, atom, offset, column, lift, boxed_ref):
    planes, count, _ = turned_ref.shape
    box = SLOT
    tiles = boxed_ref.shape[1] // (box * LANES)
    per_tile = LANES // box
    group = lane_group(column, count)
    masks = [group == r for r in range(per_tile)]
    for j in range(box):
        plane = offset + j - lift
        valid = jnp.logical_and(plane >= 0, plane < planes)
        plane = jnp.clip(plane, 0, planes - 1)
        for t in range(tiles):
            base = t * per_tile * LANES
            cells = turned_ref[plane, :, base : base + LANES]
            for r in range(1, per_tile):
                low = base + r * LANES
                cells = jnp.where(masks[r], turned_ref[plane, :, low : low + LANES], cells)
            k = j * tiles + t
            boxed_ref[:, k * LANES : (k + 1) * LANES] = jnp.where(valid, cells, jnp.zeros_like(cells))
    shifted = shifted_ref[atom, :, : boxed_ref.shape[1]]
    return lax.dot_general(boxed_ref[...], shifted, NT, preferred_element_type=f32)


def own_kernel(
    starts, turned_ref, proj_ref, coupling_ref, partial_ref, partner_ref,
    part_ref, shifted_ref, wide_coupling_ref, pair_ref, masks_ref, rows_ref, boxed_ref,
):
    atoms, nproj = proj_ref.shape[:2]
    pair_ref[...] = (partial_ref[...] + partner_ref[...]).astype(pair_ref.dtype)
    planes = turned_ref.shape[0]
    for a in range(atoms):
        offset, column = start_of(starts, a, atoms, planes, False)
        shift_projectors(proj_ref, a, a, column, rows_ref.at[a % 2], shifted_ref)
    for a in range(atoms):
        offset, column = start_of(starts, a, atoms, planes, False)
        part_ref[:, a * SLOT : (a + 1) * SLOT] = gather_atom(
            turned_ref, shifted_ref, a, offset, column, 0, boxed_ref.at[a % 2]
        )
    lane_masks([start_of(starts, a, atoms, planes, False) for a in range(atoms)], masks_ref)
    slots = atoms * SLOT
    spread = (
        lax.broadcasted_iota(jnp.int32, (nproj, slots), 0)
        == lax.broadcasted_iota(jnp.int32, (nproj, slots), 1) % SLOT
    ).astype(f32)
    exact = dict(precision=lax.Precision.HIGHEST, preferred_element_type=f32)
    right = lax.dot_general(coupling_ref[...], spread, (((0,), (0,)), ((), ())), **exact)
    both = lax.dot_general(spread, right, (((0,), (0,)), ((), ())), **exact)
    same = (
        lax.broadcasted_iota(jnp.int32, (slots, slots), 0) // SLOT
        == lax.broadcasted_iota(jnp.int32, (slots, slots), 1) // SLOT
    )
    wide_coupling_ref[...] = jnp.where(same, both, 0.0)


def carried_half(first, starts, turned_ref, proj_ref, out_ref, shifted_ref, rows_ref, boxed_ref):
    half = proj_ref.shape[0]
    planes, count, _ = turned_ref.shape
    core = lax.rem(lax.axis_index("band"), 2)
    block = core if first else 1 - core
    base = 0 if first else half
    for q in range(half):
        offset, column = start_of(starts, block * half + q, 2 * half, planes, True)
        shift_projectors(proj_ref, q, q, column, rows_ref.at[q % 2], shifted_ref)
    for q in range(half):
        offset, column = start_of(starts, block * half + q, 2 * half, planes, True)
        out_ref[:count, (base + q) * SLOT : (base + q + 1) * SLOT] = gather_atom(
            turned_ref, shifted_ref, q, offset, column, planes, boxed_ref.at[q % 2]
        )


def by_slot(table):
    core = lax.rem(lax.axis_index("band"), 2)
    return jnp.where(core == 1, pltpu.roll(table, table.shape[1] // 2, 1), table)


def first_kernel(starts, turned_ref, mine_ref, part_ref, shifted_ref, rows_ref, boxed_ref):
    part_ref[...] = jnp.zeros(part_ref.shape, f32)
    carried_half(True, starts, turned_ref, mine_ref, part_ref, shifted_ref, rows_ref, boxed_ref)


def second_kernel(
    starts, turned_ref, other_ref, half_ref, hart_ref, dens_ref,
    message_ref, shifted_ref, rows_ref, boxed_ref,
):
    count = half_ref.shape[0]
    rows = hart_ref.shape[1]
    message_ref[:count] = half_ref[...]
    carried_half(False, starts, turned_ref, other_ref, message_ref, shifted_ref, rows_ref, boxed_ref)
    message_ref[:count] = by_slot(message_ref[:count])
    message_ref[count : count + 2 * rows] = hart_ref[:2].reshape(2 * rows, LANES)
    message_ref[count + 2 * rows :] = dens_ref[0]


def weigh(coef, coupling_ref):
    return lax.dot_general(
        coef, coupling_ref[...], (((1,), (0,)), ((), ())),
        precision=lax.Precision.HIGHEST, preferred_element_type=f32,
    ).astype(bf16)


def lane_masks(spots, masks_ref):
    for slot, (_, column) in enumerate(spots):
        group = lane_group(column, SLOT)
        for r in range(masks_ref.shape[1]):
            masks_ref[slot, r] = jnp.where(group == r, 1.0, 0.0).astype(bf16)


def deposit_plane(spots, tables, masks, weighted, plane, wide_ref):
    per_tile = masks[0][0].shape[1]
    count = weighted.shape[0]
    box = SLOT
    tiles = tables[0][0].shape[2] // ((box + 1) * LANES)
    rows = tiles * per_tile
    places = []
    for first, _ in spots:
        j = plane - first
        places.append(jnp.where(jnp.logical_and(j >= 0, j < box), j, box) * (tiles * LANES))
    for t in range(tiles):
        cells = [
            table[index, :, pl.ds(pl.multiple_of(place + t * LANES, LANES), LANES)]
            for (table, index), place in zip(tables, places)
        ]
        for r in range(per_tile):
            placed = jnp.concatenate(
                [cell * ref[slot, r] for cell, (ref, slot) in zip(cells, masks)], axis=0
            )
            update = jnp.dot(weighted, placed, preferred_element_type=f32)
            row = t * per_tile + r
            wide_ref[pl.ds(row, count, stride=rows + 1), :] = pltpu.roll(
                update, (-SLOT * row) % LANES, 1
            )


def pad_rows(padded_ref, index, cells):
    rows = cells.shape[0]
    base = index * (rows + 8)
    padded_ref[base + 2 : base + 2 + rows, :] = cells
    padded_ref[base : base + 2, :] = cells[rows - 2 :]
    padded_ref[base + 2 + rows : base + 4 + rows, :] = cells[:2]


def stencil_plane(padded_ref, index, below2, below1, c, above1, above2, potential):
    rows = c.shape[0]
    base = index * (rows + 8)
    near = below1 + above1
    near = near + padded_ref[base + 1 : base + 1 + rows, :] + padded_ref[base + 3 : base + 3 + rows, :]
    near = near + pltpu.roll(c, 1, 1) + pltpu.roll(c, LANES - 1, 1)
    far = below2 + above2
    far = far + padded_ref[base : base + rows, :] + padded_ref[base + 4 : base + 4 + rows, :]
    far = far + pltpu.roll(c, 2, 1) + pltpu.roll(c, LANES - 2, 1)
    return (potential + 3.75) * c - (2.0 / 3.0) * near + (1.0 / 24.0) * far


def carried_spots(starts, atoms, planes):
    core = lax.rem(lax.axis_index("band"), 2)
    half = atoms // 2
    spots = []
    for block in (core, 1 - core):
        for q in range(half):
            offset, column = start_of(starts, block * half + q, atoms, planes, True)
            spots.append((offset - planes, column))
    return spots


def stencil_kernel(
    starts, field_ref, low_ref, high_ref, pot_ref, acc_ref, masks_ref, padded_ref
):
    count, planes, _, _ = field_ref.shape
    lane_masks(carried_spots(starts, masks_ref.shape[0], planes), masks_ref)

    def one(o, _):
        cells = (
            [low_ref[o, i].astype(f32) for i in range(2)]
            + [field_ref[o, i].astype(f32) for i in range(planes)]
            + [high_ref[o, i].astype(f32) for i in range(2)]
        )
        for i in range(planes):
            pad_rows(padded_ref, i, cells[i + 2])
            acc_ref[o, i] = stencil_plane(padded_ref, i, *cells[i : i + 5], pot_ref[i])
        return 0

    lax.fori_loop(0, count, one, 0)


def add_kernel(one_ref, other_ref, out_ref):
    out_ref[...] = one_ref[...] + other_ref[...]


def shift_kernel(cells, pot_ref, charge_ref, out_ref):
    scale = 1.0 / (6.0 + screening)
    shift = charge_ref[0:1, 0:1] * (four_pi * scale * (1.0 + 6.0 * scale) / cells)
    out_ref[...] = pot_ref[...] - shift[None]


def join_kernel(
    pair_ref, partner_ref, part_ref, hart_ref, density_ref, charge_ref, message_ref
):
    planes, rows, _ = density_ref.shape
    count = part_ref.shape[0]
    density = pair_ref[...].astype(f32) + partner_ref[...].astype(f32)
    density_ref[...] = density
    charge_ref[...] = jnp.full(charge_ref.shape, jnp.sum(density), f32)
    message_ref[:count] = part_ref[...]
    message_ref[count : count + 2 * rows] = hart_ref[planes - 2 :].reshape(2 * rows, LANES)
    message_ref[count + 2 * rows :] = density[planes - 1]


def final_kernel(
    starts, acc_ref, own_ref, mine_ref, other_ref, own_masks, prev_masks,
    part_ref, above_ref, message_ref, below_ref,
    coupling_ref, dens_ref, hart_ref, ionic_ref,
    out_ref, pot_ref, wide_ref, done_ref, sems,
):
    count, planes, rows, _ = done_ref.shape
    atoms = own_ref.shape[0]
    half = atoms // 2
    spots = [start_of(starts, a, atoms, planes, False) for a in range(atoms)]
    spots = spots + carried_spots(starts, atoms, planes)
    tables = [(own_ref, a) for a in range(atoms)]
    tables = tables + [(table, q) for table in (mine_ref, other_ref) for q in range(half)]
    masks = [(ref, a) for ref in (own_masks, prev_masks) for a in range(atoms)]
    weighted = jnp.concatenate(
        [
            weigh(part_ref[...] + above_ref[:count], coupling_ref),
            weigh(by_slot(message_ref[:count] + below_ref[:count]), coupling_ref),
        ],
        axis=1,
    )

    field = jnp.concatenate(
        [
            below_ref[count : count + 2 * rows].reshape(2, rows, LANES),
            hart_ref[...],
            above_ref[count : count + 2 * rows].reshape(2, rows, LANES),
        ],
        axis=0,
    )
    dens = jnp.concatenate(
        [
            below_ref[count + 2 * rows :].reshape(1, rows, LANES),
            dens_ref[...],
            above_ref[count + 2 * rows :].reshape(1, rows, LANES),
        ],
        axis=0,
    )
    source = four_pi * dens
    scale = 1.0 / (6.0 + screening)

    def relax(h, s):
        inner = h[1:-1]
        size = inner.shape
        flat = inner.reshape(size[0] * rows, LANES)
        across = pltpu.roll(flat, 1, 1) + pltpu.roll(flat, LANES - 1, 1)
        total = h[2:] + h[:-2] + across.reshape(size)
        total = total + pltpu.roll(inner, 1, 1) + pltpu.roll(inner, rows - 1, 1)
        return (total + s) * scale

    once = relax(field, source)
    twice = relax(once, source[1:-1])
    third = (3.0 / math.pi) * dens_ref[...]
    root = jnp.exp(jnp.log(jnp.maximum(third, 1e-37)) * (1.0 / 3.0))
    root = (2.0 * root + third / jnp.maximum(root * root, 1e-30)) * (1.0 / 3.0)
    root = jnp.where(third > 0.0, root, 0.0)
    pot_ref[...] = ionic_ref[...] + twice - root
    copies = []
    sizes = [planes // 8 * k for k in (3, 3, 1, 1)]
    base = 0
    for group, size in enumerate(sizes):
        def two(pair, _, base=base):
            for turn in range(2):
                plane = base + 2 * pair + turn
                deposit_plane(spots, tables, masks, weighted, plane, wide_ref.at[turn])
                for o in range(count):
                    low = o * (rows + 1)
                    done_ref[o, plane] = (
                        acc_ref[o, plane] + wide_ref[turn, low : low + rows, :]
                    ).astype(bf16)
            return 0

        lax.fori_loop(0, size // 2, two, 0)
        part = pl.ds(base, size)
        copies.append(
            pltpu.make_async_copy(done_ref.at[:, part], out_ref.at[:, part], sems.at[group])
        )
        copies[-1].start()
        base += size
    for copy in copies:
        copy.wait()


def around(block, axis, distance):
    count = lax.axis_size(axis)
    return lax.ppermute(block, axis, [(i, (i + distance) % count) for i in range(count)])


def swap(block, axis, mask):
    return lax.ppermute(block, axis, [(i, i ^ mask) for i in range(lax.axis_size(axis))])


def local(
    orbitals, occupations, potential_in, ionic_potential, hartree_prev, projectors, box_start, coupling
):
    count, planes, rows, lanes = orbitals.shape
    atoms, nproj, box, square = projectors.shape
    n_space = lax.axis_size("space")
    n_band = lax.axis_size("band")
    half = atoms // 2
    slots = atoms * SLOT
    cells = planes * rows * lanes
    params = pltpu.CompilerParams(vmem_limit_bytes=LIMIT << 20)

    def call(kernel, work, **kwargs):
        cost = pl.CostEstimate(flops=work * 500000, bytes_accessed=work * 1000000, transcendentals=0)
        return pl.pallas_call(kernel, compiler_params=params, cost_estimate=cost, **kwargs)

    picked = call(
        pick_kernel, 1,
        in_specs=[high_hbm()],
        out_specs=vmem(),
        out_shape=jax.ShapeDtypeStruct((half, nproj, box, square), projectors.dtype),
        scratch_shapes=[pltpu.SemaphoreType.DMA],
    )(projectors)
    mine = around(picked, "space", 1)
    other = swap(mine, "band", 1)

    groups = 4
    stride = rows + 1
    edge_shape = jax.ShapeDtypeStruct((count, 2, rows, lanes), bf16)
    partial, turned, first, last = call(
        prepare_kernel, 2,
        in_specs=[smem(), high_hbm()],
        out_specs=(vmem(),) * 4,
        out_shape=(
            jax.ShapeDtypeStruct((planes, rows, lanes), f32),
            jax.ShapeDtypeStruct((planes, count, rows * lanes), bf16),
            edge_shape,
            edge_shape,
        ),
        scratch_shapes=[
            pltpu.VMEM((count, planes, rows, lanes), bf16),
            pltpu.VMEM((2, count * stride, lanes), f32),
            pltpu.SemaphoreType.DMA((groups,)),
        ],
    )(occupations, orbitals)

    shifted_shape = jax.ShapeDtypeStruct((atoms, SLOT, (box + 1) * square), bf16)
    gather_scratch = [
        pltpu.VMEM((2, square // lanes, SLOT * (box + 1), lanes), f32),
        pltpu.VMEM((2, count, box * square), bf16),
    ]
    mask_shape = jax.ShapeDtypeStruct((atoms, lanes // SLOT, SLOT, lanes), bf16)
    own_part, own_shifted, wide_coupling, pair, own_masks = call(
        own_kernel, 4,
        in_specs=[smem()] + [vmem()] * 5,
        out_specs=(vmem(),) * 5,
        out_shape=(
            jax.ShapeDtypeStruct((count, slots), f32),
            shifted_shape,
            jax.ShapeDtypeStruct((slots, slots), f32),
            jax.ShapeDtypeStruct((planes, rows, lanes), bf16),
            mask_shape,
        ),
        scratch_shapes=gather_scratch,
    )(box_start, turned, projectors, coupling, partial, swap(partial, "band", 1))

    mask = 2
    while 2 * mask < n_band:
        pair = (pair.astype(f32) + swap(pair, "band", mask).astype(f32)).astype(bf16)
        mask *= 2
    message_shape = jax.ShapeDtypeStruct((count + 3 * rows, lanes), f32)
    density, charge, below = call(
        join_kernel, 1,
        in_specs=[vmem()] * 4,
        out_specs=(vmem(),) * 3,
        out_shape=(
            jax.ShapeDtypeStruct((planes, rows, lanes), f32),
            jax.ShapeDtypeStruct((8, lanes), f32),
            message_shape,
        ),
    )(pair, swap(pair, "band", mask), own_part, hartree_prev)
    below = around(below, "space", 1)
    low = around(last, "space", 1)
    high = around(first, "space", -1)
    mask = 1
    while mask < n_space:
        charge = call(
            add_kernel, 1,
            in_specs=[vmem(), vmem()],
            out_specs=vmem(),
            out_shape=jax.ShapeDtypeStruct((8, lanes), f32),
        )(charge, swap(charge, "space", mask))
        mask *= 2

    half_shape = jax.ShapeDtypeStruct((half, SLOT, (box + 1) * square), bf16)
    prev_half, mine_shifted = call(
        first_kernel, 2,
        in_specs=[smem()] + [vmem()] * 2,
        out_specs=(vmem(), vmem()),
        out_shape=(jax.ShapeDtypeStruct((count, slots), f32), half_shape),
        scratch_shapes=gather_scratch,
    )(box_start, turned, mine)
    message, other_shifted = call(
        second_kernel, 2,
        in_specs=[smem()] + [vmem()] * 5,
        out_specs=(vmem(), vmem()),
        out_shape=(message_shape, half_shape),
        scratch_shapes=gather_scratch,
    )(box_start, turned, other, prev_half, hartree_prev, density)

    above = around(message, "space", -1)

    acc, prev_masks = call(
        stencil_kernel, 4,
        in_specs=[smem()] + [vmem()] * 4,
        out_specs=(vmem(), vmem()),
        out_shape=(jax.ShapeDtypeStruct((count, planes, rows, lanes), f32), mask_shape),
        scratch_shapes=[pltpu.VMEM((planes * (rows + 8), lanes), f32)],
    )(box_start, orbitals, low, high, potential_in)

    applied, potential = call(
        final_kernel, 6,
        in_specs=[smem()] + [vmem()] * 14,
        out_specs=(hbm(), vmem()),
        out_shape=(
            jax.ShapeDtypeStruct((count, planes, rows, lanes), bf16),
            jax.ShapeDtypeStruct((planes, rows, lanes), f32),
        ),
        scratch_shapes=[
            pltpu.VMEM((2, count * stride, lanes), f32),
            pltpu.VMEM((count, planes, rows, lanes), bf16),
            pltpu.SemaphoreType.DMA((groups,)),
        ],
    )(
        box_start, acc, own_shifted, mine_shifted, other_shifted, own_masks, prev_masks, own_part, above, message, below,
        wide_coupling, density, hartree_prev, ionic_potential,
    )
    potential = call(
        functools.partial(shift_kernel, float(cells * n_space)), 1,
        in_specs=[vmem(), vmem()],
        out_specs=vmem(),
        out_shape=jax.ShapeDtypeStruct((planes, rows, lanes), f32),
    )(potential, charge)
    return applied, potential


def solution(mesh):
    placed = (
        P("band", "space", None, None),
        P("band"),
        P("space", None, None),
        P("space", None, None),
        P("space", None, None),
        P("space", None, None, None),
        P(),
        P(),
    )

    return jax.shard_map(
        local,
        mesh=mesh,
        in_specs=placed,
        out_specs=(P("band", "space", None, None), P("space", None, None)),
        check_vma=False,
    )
```

```python
import functools
import math

import jax
import jax.numpy as jnp
from jax import lax
from jax.experimental import pallas as pl
from jax.experimental.pallas import tpu as pltpu
from jax.sharding import PartitionSpec as P


LANES = 128
SLOT = 16
LIMIT = 24

screening = 0.25
four_pi = 4.0 * math.pi
f32 = jnp.float32
bf16 = jnp.bfloat16


def vmem():
    return pl.BlockSpec(memory_space=pltpu.VMEM)


def smem():
    return pl.BlockSpec(memory_space=pltpu.SMEM)


def high_hbm():
    return pl.BlockSpec(memory_space=pltpu.HBM)


def hbm():
    return pl.BlockSpec(memory_space=pl.ANY)


NT = (((1,), (1,)), ((), ()))


def start_of(starts, atom, atoms, planes, carried):
    domain = lax.axis_index("space")
    if carried:
        count = lax.axis_size("space")
        domain = lax.rem(domain + (count - 1), count)
    index = domain * atoms + atom
    return lax.rem(starts[0, index], planes), starts[2, index]


def pick_kernel(proj_ref, out_ref, sem):
    half = out_ref.shape[0]
    core = lax.rem(lax.axis_index("band"), 2)
    copy = pltpu.make_async_copy(proj_ref.at[pl.ds(core * half, half)], out_ref, sem)
    copy.start()
    copy.wait()


def density_kernel(occ, field_ref, _, density_ref):
    count, planes, rows, _ = field_ref.shape
    for plane in range(planes):
        total = jnp.zeros((rows, LANES), f32)
        for o in range(count):
            cells = field_ref[o, plane].astype(f32)
            total = total + (occ[o] * cells) * cells
        density_ref[plane] = total


def pair_kernel(partial_ref, partner_ref, pair_ref):
    pair_ref[...] = (partial_ref[...] + partner_ref[...]).astype(pair_ref.dtype)


def turn_kernel(field_ref, turned_ref, first_ref, last_ref, wide_ref):
    count, planes, rows, _ = field_ref.shape
    stride = rows + 1
    for plane in range(planes):
        turn = plane % 2
        for o in range(count):
            wide_ref[turn, o * stride : o * stride + rows, :] = field_ref[o, plane].astype(f32)
        turned_ref[plane] = jnp.concatenate(
            [
                pltpu.roll(
                    wide_ref[turn, pl.ds(r, count, stride=stride), :], (SLOT * r) % LANES, 1
                )
                for r in range(rows)
            ],
            axis=1,
        ).astype(bf16)
    first_ref[...] = field_ref[:, :2]
    last_ref[...] = field_ref[:, planes - 2 :]


def shift_projectors(raw_ref, index, atom, column, rows_ref, shifted_ref):
    nproj, box, square = raw_ref.shape[1:]
    stride = box + 1
    tiles = square // LANES
    for p in range(SLOT):
        if p < nproj:
            cells = raw_ref[index, p].astype(f32)
        else:
            cells = jnp.zeros((box, square), f32)
        for t in range(tiles):
            rows_ref[t, p * stride : p * stride + box, :] = cells[:, t * LANES : (t + 1) * LANES]
    for j in range(box):
        for t in range(tiles):
            cells = rows_ref[t, pl.ds(j, SLOT, stride=stride), :].astype(bf16)
            k = j * tiles + t
            shifted_ref[atom, :, k * LANES : (k + 1) * LANES] = pltpu.roll(cells, column, 1)
    shifted_ref[atom, :, box * square :] = jnp.zeros((SLOT, square), bf16)


def lane_group(column, height):
    lane = lax.broadcasted_iota(jnp.int32, (height, LANES), 1)
    return lax.shift_right_logical(jnp.bitwise_and(lane - column + LANES, LANES - 1), 4)


def gather_atom(turned_ref, shifted_ref, atom, offset, column, lift, boxed_ref):
    planes, count, _ = turned_ref.shape
    box = SLOT
    tiles = boxed_ref.shape[1] // (box * LANES)
    per_tile = LANES // box
    group = lane_group(column, count)
    masks = [group == r for r in range(per_tile)]
    for j in range(box):
        plane = offset + j - lift
        valid = jnp.logical_and(plane >= 0, plane < planes)
        plane = jnp.clip(plane, 0, planes - 1)
        for t in range(tiles):
            base = t * per_tile * LANES
            cells = turned_ref[plane, :, base : base + LANES]
            for r in range(1, per_tile):
                low = base + r * LANES
                cells = jnp.where(masks[r], turned_ref[plane, :, low : low + LANES], cells)
            k = j * tiles + t
            boxed_ref[:, k * LANES : (k + 1) * LANES] = jnp.where(valid, cells, jnp.zeros_like(cells))
    shifted = shifted_ref[atom, :, : boxed_ref.shape[1]]
    return lax.dot_general(boxed_ref[...], shifted, NT, preferred_element_type=f32)


def own_kernel(
    starts, turned_ref, proj_ref, coupling_ref,
    part_ref, shifted_ref, wide_coupling_ref, masks_ref, rows_ref, boxed_ref,
):
    atoms, nproj = proj_ref.shape[:2]
    planes = turned_ref.shape[0]
    for a in range(atoms):
        offset, column = start_of(starts, a, atoms, planes, False)
        shift_projectors(proj_ref, a, a, column, rows_ref.at[a % 2], shifted_ref)
    for a in range(atoms):
        offset, column = start_of(starts, a, atoms, planes, False)
        part_ref[:, a * SLOT : (a + 1) * SLOT] = gather_atom(
            turned_ref, shifted_ref, a, offset, column, 0, boxed_ref.at[a % 2]
        )
    lane_masks([start_of(starts, a, atoms, planes, False) for a in range(atoms)], masks_ref)
    slots = atoms * SLOT
    spread = (
        lax.broadcasted_iota(jnp.int32, (nproj, slots), 0)
        == lax.broadcasted_iota(jnp.int32, (nproj, slots), 1) % SLOT
    ).astype(f32)
    exact = dict(precision=lax.Precision.HIGHEST, preferred_element_type=f32)
    right = lax.dot_general(coupling_ref[...], spread, (((0,), (0,)), ((), ())), **exact)
    both = lax.dot_general(spread, right, (((0,), (0,)), ((), ())), **exact)
    same = (
        lax.broadcasted_iota(jnp.int32, (slots, slots), 0) // SLOT
        == lax.broadcasted_iota(jnp.int32, (slots, slots), 1) // SLOT
    )
    wide_coupling_ref[...] = jnp.where(same, both, 0.0)


def carried_half(first, starts, turned_ref, proj_ref, out_ref, shifted_ref, rows_ref, boxed_ref):
    half = proj_ref.shape[0]
    planes, count, _ = turned_ref.shape
    core = lax.rem(lax.axis_index("band"), 2)
    block = core if first else 1 - core
    base = 0 if first else half
    for q in range(half):
        offset, column = start_of(starts, block * half + q, 2 * half, planes, True)
        shift_projectors(proj_ref, q, q, column, rows_ref.at[q % 2], shifted_ref)
    for q in range(half):
        offset, column = start_of(starts, block * half + q, 2 * half, planes, True)
        out_ref[:count, (base + q) * SLOT : (base + q + 1) * SLOT] = gather_atom(
            turned_ref, shifted_ref, q, offset, column, planes, boxed_ref.at[q % 2]
        )


def by_slot(table):
    core = lax.rem(lax.axis_index("band"), 2)
    return jnp.where(core == 1, pltpu.roll(table, table.shape[1] // 2, 1), table)


def first_kernel(starts, turned_ref, mine_ref, part_ref, shifted_ref, rows_ref, boxed_ref):
    part_ref[...] = jnp.zeros(part_ref.shape, f32)
    carried_half(True, starts, turned_ref, mine_ref, part_ref, shifted_ref, rows_ref, boxed_ref)


def second_kernel(
    starts, turned_ref, other_ref, half_ref, hart_ref, dens_ref,
    message_ref, shifted_ref, rows_ref, boxed_ref,
):
    count = half_ref.shape[0]
    rows = hart_ref.shape[1]
    message_ref[:count] = half_ref[...]
    carried_half(False, starts, turned_ref, other_ref, message_ref, shifted_ref, rows_ref, boxed_ref)
    message_ref[:count] = by_slot(message_ref[:count])
    message_ref[count : count + 2 * rows] = hart_ref[:2].reshape(2 * rows, LANES)
    message_ref[count + 2 * rows :] = dens_ref[0]


def weigh(coef, coupling_ref):
    return lax.dot_general(
        coef, coupling_ref[...], (((1,), (0,)), ((), ())),
        precision=lax.Precision.HIGHEST, preferred_element_type=f32,
    ).astype(bf16)


def lane_masks(spots, masks_ref):
    for slot, (_, column) in enumerate(spots):
        group = lane_group(column, SLOT)
        for r in range(masks_ref.shape[1]):
            masks_ref[slot, r] = jnp.where(group == r, 1.0, 0.0).astype(bf16)


def deposit_plane(spots, tables, masks, weighted, plane, wide_ref):
    per_tile = masks[0][0].shape[1]
    count = weighted.shape[0]
    box = SLOT
    tiles = tables[0][0].shape[2] // ((box + 1) * LANES)
    rows = tiles * per_tile
    places = []
    for first, _ in spots:
        j = plane - first
        places.append(jnp.where(jnp.logical_and(j >= 0, j < box), j, box) * (tiles * LANES))
    for t in range(tiles):
        cells = [
            table[index, :, pl.ds(pl.multiple_of(place + t * LANES, LANES), LANES)]
            for (table, index), place in zip(tables, places)
        ]
        for r in range(per_tile):
            placed = jnp.concatenate(
                [cell * ref[slot, r] for cell, (ref, slot) in zip(cells, masks)], axis=0
            )
            update = jnp.dot(weighted, placed, preferred_element_type=f32)
            row = t * per_tile + r
            wide_ref[pl.ds(row, count, stride=rows + 1), :] = pltpu.roll(
                update, (-SLOT * row) % LANES, 1
            )


def pad_rows(padded_ref, index, cells):
    rows = cells.shape[0]
    base = index * (rows + 8)
    padded_ref[base + 2 : base + 2 + rows, :] = cells
    padded_ref[base : base + 2, :] = cells[rows - 2 :]
    padded_ref[base + 2 + rows : base + 4 + rows, :] = cells[:2]


def stencil_plane(padded_ref, index, below2, below1, c, above1, above2, potential):
    rows = c.shape[0]
    base = index * (rows + 8)
    near = below1 + above1
    near = near + padded_ref[base + 1 : base + 1 + rows, :] + padded_ref[base + 3 : base + 3 + rows, :]
    near = near + pltpu.roll(c, 1, 1) + pltpu.roll(c, LANES - 1, 1)
    far = below2 + above2
    far = far + padded_ref[base : base + rows, :] + padded_ref[base + 4 : base + 4 + rows, :]
    far = far + pltpu.roll(c, 2, 1) + pltpu.roll(c, LANES - 2, 1)
    return (potential + 3.75) * c - (2.0 / 3.0) * near + (1.0 / 24.0) * far


def carried_spots(starts, atoms, planes):
    core = lax.rem(lax.axis_index("band"), 2)
    half = atoms // 2
    spots = []
    for block in (core, 1 - core):
        for q in range(half):
            offset, column = start_of(starts, block * half + q, atoms, planes, True)
            spots.append((offset - planes, column))
    return spots


def stencil_kernel(
    starts, field_ref, low_ref, high_ref, pot_ref, acc_ref, masks_ref, padded_ref
):
    count, planes, _, _ = field_ref.shape
    lane_masks(carried_spots(starts, masks_ref.shape[0], planes), masks_ref)

    def one(o, _):
        cells = (
            [low_ref[o, i].astype(f32) for i in range(2)]
            + [field_ref[o, i].astype(f32) for i in range(planes)]
            + [high_ref[o, i].astype(f32) for i in range(2)]
        )
        for i in range(planes):
            pad_rows(padded_ref, i, cells[i + 2])
            acc_ref[o, i] = stencil_plane(padded_ref, i, *cells[i : i + 5], pot_ref[i])
        return 0

    lax.fori_loop(0, count, one, 0)


def add_kernel(one_ref, other_ref, out_ref):
    out_ref[...] = one_ref[...] + other_ref[...]


def shift_kernel(cells, pot_ref, charge_ref, out_ref):
    scale = 1.0 / (6.0 + screening)
    shift = charge_ref[0:1, 0:1] * (four_pi * scale * (1.0 + 6.0 * scale) / cells)
    out_ref[...] = pot_ref[...] - shift[None]


def join_kernel(
    pair_ref, partner_ref, part_ref, hart_ref, density_ref, charge_ref, message_ref
):
    planes, rows, _ = density_ref.shape
    count = part_ref.shape[0]
    density = pair_ref[...].astype(f32) + partner_ref[...].astype(f32)
    density_ref[...] = density
    charge_ref[...] = jnp.full(charge_ref.shape, jnp.sum(density), f32)
    message_ref[:count] = part_ref[...]
    message_ref[count : count + 2 * rows] = hart_ref[planes - 2 :].reshape(2 * rows, LANES)
    message_ref[count + 2 * rows :] = density[planes - 1]


def final_kernel(
    starts, acc_ref, own_ref, mine_ref, other_ref, own_masks, prev_masks,
    part_ref, above_ref, message_ref, below_ref,
    coupling_ref, dens_ref, hart_ref, ionic_ref,
    out_ref, pot_ref, wide_ref, done_ref, sems,
):
    count, planes, rows, _ = done_ref.shape
    atoms = own_ref.shape[0]
    half = atoms // 2
    spots = [start_of(starts, a, atoms, planes, False) for a in range(atoms)]
    spots = spots + carried_spots(starts, atoms, planes)
    tables = [(own_ref, a) for a in range(atoms)]
    tables = tables + [(table, q) for table in (mine_ref, other_ref) for q in range(half)]
    masks = [(ref, a) for ref in (own_masks, prev_masks) for a in range(atoms)]
    weighted = jnp.concatenate(
        [
            weigh(part_ref[...] + above_ref[:count], coupling_ref),
            weigh(by_slot(message_ref[:count] + below_ref[:count]), coupling_ref),
        ],
        axis=1,
    )

    field = jnp.concatenate(
        [
            below_ref[count : count + 2 * rows].reshape(2, rows, LANES),
            hart_ref[...],
            above_ref[count : count + 2 * rows].reshape(2, rows, LANES),
        ],
        axis=0,
    )
    dens = jnp.concatenate(
        [
            below_ref[count + 2 * rows :].reshape(1, rows, LANES),
            dens_ref[...],
            above_ref[count + 2 * rows :].reshape(1, rows, LANES),
        ],
        axis=0,
    )
    source = four_pi * dens
    scale = 1.0 / (6.0 + screening)

    def relax(h, s):
        inner = h[1:-1]
        size = inner.shape
        flat = inner.reshape(size[0] * rows, LANES)
        across = pltpu.roll(flat, 1, 1) + pltpu.roll(flat, LANES - 1, 1)
        total = h[2:] + h[:-2] + across.reshape(size)
        total = total + pltpu.roll(inner, 1, 1) + pltpu.roll(inner, rows - 1, 1)
        return (total + s) * scale

    once = relax(field, source)
    twice = relax(once, source[1:-1])
    third = (3.0 / math.pi) * dens_ref[...]
    root = jnp.exp(jnp.log(jnp.maximum(third, 1e-37)) * (1.0 / 3.0))
    root = (2.0 * root + third / jnp.maximum(root * root, 1e-30)) * (1.0 / 3.0)
    root = jnp.where(third > 0.0, root, 0.0)
    pot_ref[...] = ionic_ref[...] + twice - root
    copies = []
    sizes = [planes // 8 * k for k in (3, 3, 1, 1)]
    base = 0
    for group, size in enumerate(sizes):
        def two(pair, _, base=base):
            for turn in range(2):
                plane = base + 2 * pair + turn
                deposit_plane(spots, tables, masks, weighted, plane, wide_ref.at[turn])
                for o in range(count):
                    low = o * (rows + 1)
                    done_ref[o, plane] = (
                        acc_ref[o, plane] + wide_ref[turn, low : low + rows, :]
                    ).astype(bf16)
            return 0

        lax.fori_loop(0, size // 2, two, 0)
        part = pl.ds(base, size)
        copies.append(
            pltpu.make_async_copy(done_ref.at[:, part], out_ref.at[:, part], sems.at[group])
        )
        copies[-1].start()
        base += size
    for copy in copies:
        copy.wait()


def around(block, axis, distance):
    count = lax.axis_size(axis)
    return lax.ppermute(block, axis, [(i, (i + distance) % count) for i in range(count)])


def swap(block, axis, mask):
    return lax.ppermute(block, axis, [(i, i ^ mask) for i in range(lax.axis_size(axis))])


def local(
    orbitals, occupations, potential_in, ionic_potential, hartree_prev, projectors, box_start, coupling
):
    count, planes, rows, lanes = orbitals.shape
    atoms, nproj, box, square = projectors.shape
    n_space = lax.axis_size("space")
    n_band = lax.axis_size("band")
    half = atoms // 2
    slots = atoms * SLOT
    cells = planes * rows * lanes
    params = pltpu.CompilerParams(vmem_limit_bytes=LIMIT << 20)

    def call(kernel, work, **kwargs):
        cost = pl.CostEstimate(flops=work * 500000, bytes_accessed=work * 1000000, transcendentals=0)
        return pl.pallas_call(kernel, compiler_params=params, cost_estimate=cost, **kwargs)

    picked = call(
        pick_kernel, 1,
        in_specs=[high_hbm()],
        out_specs=vmem(),
        out_shape=jax.ShapeDtypeStruct((half, nproj, box, square), projectors.dtype),
        scratch_shapes=[pltpu.SemaphoreType.DMA],
    )(projectors)
    mine = around(picked, "space", 1)
    other = swap(mine, "band", 1)

    groups = 4
    stride = rows + 1
    edge_shape = jax.ShapeDtypeStruct((count, 2, rows, lanes), bf16)
    turned, first, last = call(
        turn_kernel, 2,
        in_specs=[vmem()],
        out_specs=(vmem(),) * 3,
        out_shape=(
            jax.ShapeDtypeStruct((planes, count, rows * lanes), bf16),
            edge_shape,
            edge_shape,
        ),
        scratch_shapes=[pltpu.VMEM((2, count * stride, lanes), f32)],
    )(orbitals)
    partial = call(
        density_kernel, 1,
        in_specs=[smem(), vmem(), hbm()],
        out_specs=vmem(),
        out_shape=jax.ShapeDtypeStruct((planes, rows, lanes), f32),
    )(occupations, orbitals, last)

    shifted_shape = jax.ShapeDtypeStruct((atoms, SLOT, (box + 1) * square), bf16)
    gather_scratch = [
        pltpu.VMEM((2, square // lanes, SLOT * (box + 1), lanes), f32),
        pltpu.VMEM((2, count, box * square), bf16),
    ]
    mask_shape = jax.ShapeDtypeStruct((atoms, lanes // SLOT, SLOT, lanes), bf16)
    own_part, own_shifted, wide_coupling, own_masks = call(
        own_kernel, 4,
        in_specs=[smem()] + [vmem()] * 3,
        out_specs=(vmem(),) * 4,
        out_shape=(
            jax.ShapeDtypeStruct((count, slots), f32),
            shifted_shape,
            jax.ShapeDtypeStruct((slots, slots), f32),
            mask_shape,
        ),
        scratch_shapes=gather_scratch,
    )(box_start, turned, projectors, coupling)
    pair = call(
        pair_kernel, 1,
        in_specs=[vmem(), vmem()],
        out_specs=vmem(),
        out_shape=jax.ShapeDtypeStruct((planes, rows, lanes), bf16),
    )(partial, swap(partial, "band", 1))

    mask = 2
    while 2 * mask < n_band:
        pair = (pair.astype(f32) + swap(pair, "band", mask).astype(f32)).astype(bf16)
        mask *= 2
    message_shape = jax.ShapeDtypeStruct((count + 3 * rows, lanes), f32)
    density, charge, below = call(
        join_kernel, 1,
        in_specs=[vmem()] * 4,
        out_specs=(vmem(),) * 3,
        out_shape=(
            jax.ShapeDtypeStruct((planes, rows, lanes), f32),
            jax.ShapeDtypeStruct((8, lanes), f32),
            message_shape,
        ),
    )(pair, swap(pair, "band", mask), own_part, hartree_prev)
    below = around(below, "space", 1)
    low = around(last, "space", 1)
    high = around(first, "space", -1)
    mask = 1
    while mask < n_space:
        charge = call(
            add_kernel, 1,
            in_specs=[vmem(), vmem()],
            out_specs=vmem(),
            out_shape=jax.ShapeDtypeStruct((8, lanes), f32),
        )(charge, swap(charge, "space", mask))
        mask *= 2

    half_shape = jax.ShapeDtypeStruct((half, SLOT, (box + 1) * square), bf16)
    prev_half, mine_shifted = call(
        first_kernel, 2,
        in_specs=[smem()] + [vmem()] * 2,
        out_specs=(vmem(), vmem()),
        out_shape=(jax.ShapeDtypeStruct((count, slots), f32), half_shape),
        scratch_shapes=gather_scratch,
    )(box_start, turned, mine)
    message, other_shifted = call(
        second_kernel, 2,
        in_specs=[smem()] + [vmem()] * 5,
        out_specs=(vmem(), vmem()),
        out_shape=(message_shape, half_shape),
        scratch_shapes=gather_scratch,
    )(box_start, turned, other, prev_half, hartree_prev, density)

    above = around(message, "space", -1)

    acc, prev_masks = call(
        stencil_kernel, 4,
        in_specs=[smem()] + [vmem()] * 4,
        out_specs=(vmem(), vmem()),
        out_shape=(jax.ShapeDtypeStruct((count, planes, rows, lanes), f32), mask_shape),
        scratch_shapes=[pltpu.VMEM((planes * (rows + 8), lanes), f32)],
    )(box_start, orbitals, low, high, potential_in)

    applied, potential = call(
        final_kernel, 6,
        in_specs=[smem()] + [vmem()] * 14,
        out_specs=(hbm(), vmem()),
        out_shape=(
            jax.ShapeDtypeStruct((count, planes, rows, lanes), bf16),
            jax.ShapeDtypeStruct((planes, rows, lanes), f32),
        ),
        scratch_shapes=[
            pltpu.VMEM((2, count * stride, lanes), f32),
            pltpu.VMEM((count, planes, rows, lanes), bf16),
            pltpu.SemaphoreType.DMA((groups,)),
        ],
    )(
        box_start, acc, own_shifted, mine_shifted, other_shifted, own_masks, prev_masks, own_part, above, message, below,
        wide_coupling, density, hartree_prev, ionic_potential,
    )
    potential = call(
        functools.partial(shift_kernel, float(cells * n_space)), 1,
        in_specs=[vmem(), vmem()],
        out_specs=vmem(),
        out_shape=jax.ShapeDtypeStruct((planes, rows, lanes), f32),
    )(potential, charge)
    return applied, potential


def solution(mesh):
    placed = (
        P("band", "space", None, None),
        P("band"),
        P("space", None, None),
        P("space", None, None),
        P("space", None, None),
        P("space", None, None, None),
        P(),
        P(),
    )

    return jax.shard_map(
        local,
        mesh=mesh,
        in_specs=placed,
        out_specs=(P("band", "space", None, None), P("space", None, None)),
        check_vma=False,
    )
```
